256 devices in a mesh: rays: 64 (over z_hi, y, x), planes: 4 (over z_lo, core).
Axes of the slice: x: 4, y: 4, z: 8 (z_hi: 4, z_lo: 2; z = z_hi * 2 + z_lo), core: 2. Of those that a mesh axis runs over, the one named last changes fastest.
Arguments:
- tile_density: bfloat16 [4, 256, 128, 128], P(None, 'rays', 'planes'), may hold values from -6 to 6
- long_maps: bfloat16 [64, 4, 512, 2, 512], P('rays'), may hold values from -1.796875 to 1.796875
- map_owner: int32 [4], replicated, may hold values from 0 to 63
- tile_lists: int32 [64, 4, 64], replicated, may hold values from 0 to 255, as said below
- block_slots: int32 [4, 4096], P(None, ('rays', 'planes')), may hold values from 0 to 63
- block_windows: int32 [4, 2, 4096], P(None, None, ('rays', 'planes')), may hold values from 0 to 384
- fine_cells: int32 [4, 2, 2097152], P(None, None, ('rays', 'planes')), may hold values from 0 to 126
- long_cells: int32 [4, 2, 2097152], P(None, None, ('rays', 'planes')), may hold values from 0 to 126
- fractions: float32 [4, 4, 2097152], P(None, None, ('rays', 'planes')), may hold values from 0 to 1
Outputs:
- deflection: float32 [4, 2, 2097152], P(None, None, ('rays', 'planes'))
- source_shift: float32 [2, 2097152], P(None, ('rays', 'planes'))
The draws below stay inside these ranges and needn't reach their ends.
Inputs may be any that keep to these rules, and one draw needn't show every extreme that they name: `tile_lists`: tile t belongs to owner t // 4. In each list of one bundle and plane at most 2 entries name tiles of one owner, and some owner has exactly 2 entries in every such list; entries may repeat.
All inputs are finite; a program needn't handle non-finite values.
Results may differ from the reference program's by a relative error of at most 0.0064.
Values may be sent and summed in bfloat16 or wider, within the bound.
No kernel may reach another device: no remote copies, remote signals or barrier semaphores. Data moves between devices by JAX's collectives and lax.ppermute only.
A program may use at most 128 MiB of HBM per device.

```python
import jax
import jax.numpy as jnp
from jax import lax

TS = 128
M = 512
PLANES = 4
TILES = 256
LIST = 64
RAYS_DEV = 8192
BLK = 512
RATIO = 16
TILE_DEV = 4
CAP = 2
RAYS = 2097152
NBLK = 4096
N_RAYS = 64
N_PLANES = 4


def draw_tile_lists(key, part):
    slot_count = N_RAYS * CAP

    def draw_single(single_key, flat_index):
        key_order, key_shuffle, key_local = jax.random.split(single_key, 3)
        shuffled = jax.random.permutation(key_order, slot_count)
        position = jnp.argsort(shuffled, stable=True).astype(jnp.int32)
        owner_ids = jnp.arange(slot_count, dtype=jnp.int32) // CAP
        bundle = flat_index // PLANES
        plane_index = flat_index % PLANES
        target = (bundle * 5 + plane_index * 3) % N_RAYS
        scores = position + jnp.where(owner_ids == target, 0, slot_count)
        chosen = jnp.argsort(scores, stable=True)[:LIST].astype(jnp.int32)
        chosen = jax.random.permutation(key_shuffle, chosen)
        local_index = jax.random.randint(key_local, (LIST,), 0, TILE_DEV, dtype=jnp.int32)
        return chosen // CAP * TILE_DEV + local_index
    key_list = jax.random.split(key, N_RAYS * PLANES)
    drawn = jax.vmap(draw_single)(key_list, jnp.arange(N_RAYS * PLANES, dtype=jnp.int32))
    return drawn.reshape(N_RAYS, PLANES, LIST).astype(jnp.int32)


def with_ends(values, own_key, low, top_value):
    extent = values.shape
    place = [jax.random.randint(jax.random.fold_in(own_key, axis), (), 0, extent[axis]) for axis in range(len(extent))]
    values = values.at[tuple(place)].set(low)
    longest = extent.index(max(extent))
    place[longest] = (place[longest] + 1) % extent[longest]
    return values.at[tuple(place)].set(top_value)


def steps_of(own_key, dims, pieces, low, top_value):
    level = 1.0
    for dim, parts in pieces:
        steps = jax.random.uniform(jax.random.fold_in(jax.random.fold_in(own_key, 6), dim), (parts,), jnp.float32, low / len(pieces), top_value / len(pieces))
        level = level * jnp.repeat(jnp.exp(steps), dims[dim] // parts).reshape((-1,) + (1,) * (len(dims) - 1 - dim))
    return level


def centred(stream_key, dims, spread, most, shards=(), kind=jnp.bfloat16):
    result = jax.random.normal(stream_key, dims, jnp.float32) * spread
    if len(shards) > 0:
        result = steps_of(stream_key, dims, shards, -0.22, 0.18) * result
    return jnp.clip(result, min=-most, max=most).astype(kind)


def setup_inputs(seed: int = 0) -> dict:
    streams_of = jax.random.split(jax.random.key(seed), 10)
    tile_density = centred(streams_of[0], (PLANES, TILES, TS, TS), 1.0, 6.0, ((1, 64), (2, 4)))
    long_maps = centred(streams_of[1], (N_RAYS, PLANES, M, 2, M), 0.3, 1.796875, ((0, 64),))
    map_owner = with_ends(jax.random.randint(streams_of[2], (PLANES,), 0, N_RAYS), jax.random.fold_in(streams_of[2], 1), 0, N_RAYS - 1).astype(jnp.int32)
    tile_lists = draw_tile_lists(jax.random.fold_in(streams_of[9], 71), 0)
    block_slots = with_ends(jax.random.randint(streams_of[4], (PLANES, NBLK), 0, LIST), jax.random.fold_in(streams_of[4], 1), 0, LIST - 1).astype(jnp.int32)
    block_windows = with_ends(jax.random.randint(streams_of[5], (PLANES, 2, NBLK), 0, M - TS + 1), jax.random.fold_in(streams_of[5], 1), 0, M - TS).astype(jnp.int32)
    fine_cells = with_ends(jax.random.randint(streams_of[6], (PLANES, 2, RAYS), 0, TS - 1), jax.random.fold_in(streams_of[6], 1), 0, (TS - 1) - 1).astype(jnp.int32)
    long_cells = with_ends(jax.random.randint(streams_of[7], (PLANES, 2, RAYS), 0, TS - 1), jax.random.fold_in(streams_of[7], 1), 0, (TS - 1) - 1).astype(jnp.int32)
    fractions = jnp.clip(1.0 * jax.random.uniform(streams_of[8], (PLANES, 4, RAYS), jnp.float32) ** steps_of(streams_of[8], (PLANES, 4, RAYS), ((2, 256),), -0.2, 0.2), 0.0, 1.0)
    return dict(tile_density=tile_density, long_maps=long_maps, map_owner=map_owner, tile_lists=tile_lists, block_slots=block_slots, block_windows=block_windows, fine_cells=fine_cells, long_cells=long_cells, fractions=fractions)


def kernel_tables(side):
    indices = jnp.arange(side, dtype=jnp.int32)
    offset = (indices[:, None] - indices[None, :]).astype(jnp.float32)
    tap_offsets = jnp.arange(-6, 7, dtype=jnp.int32).astype(jnp.float32)
    tap_total = jnp.sum(jnp.exp(-tap_offsets * tap_offsets / 8.0))
    inside = jnp.abs(offset) <= 6.0
    weight = jnp.where(inside, jnp.exp(-offset * offset / 8.0), 0.0) / tap_total
    smooth_table = weight.astype(jnp.bfloat16)
    slope_table = (6.0 * offset * weight / 4.0).astype(jnp.bfloat16)
    return smooth_table, slope_table


def rounded(values):
    return lax.optimization_barrier(values.astype(jnp.bfloat16)).astype(jnp.float32)


def convolve(density, smooth_table, slope_table):
    side = density.shape[1]
    right_table = jnp.concatenate([smooth_table.T, slope_table.T], axis=1).astype(jnp.float32)
    partial_value = rounded(jnp.einsum("lij,jk->lik", density.astype(jnp.float32), right_table))
    along_rows = jnp.einsum("ij,ljk->lik", slope_table.astype(jnp.float32), partial_value[:, :, :side])
    along_cols = jnp.einsum("ij,ljk->lik", smooth_table.astype(jnp.float32), partial_value[:, :, side:])
    return jnp.concatenate([along_rows, along_cols], axis=2).astype(jnp.bfloat16)


def interpolate(lookup, cell_row, cell_col, frac_row, frac_col):
    side = lookup.shape[1]
    positions = jnp.arange(side, dtype=jnp.int32)
    row_weight = jnp.where(positions == cell_row[..., None], 1.0 - frac_row[..., None], 0.0)
    row_weight = row_weight + jnp.where(positions == cell_row[..., None] + 1, frac_row[..., None], 0.0)
    col_weight = jnp.where(positions == cell_col[..., None], 1.0 - frac_col[..., None], 0.0)
    col_weight = col_weight + jnp.where(positions == cell_col[..., None] + 1, frac_col[..., None], 0.0)
    row_values = jnp.einsum("bns,bsk->bnk", rounded(row_weight), lookup.astype(jnp.float32))
    along_x = jnp.sum(row_values[..., :side] * col_weight, axis=-1)
    along_y = jnp.sum(row_values[..., side:] * col_weight, axis=-1)
    return along_x, along_y


def map_windows(map_full, starts, side):
    def one_window(row_start, col_start):
        window = lax.dynamic_slice(map_full, (row_start, jnp.int32(0), col_start), (side, 2, side))
        return window.reshape(side, 2 * side)
    return jax.vmap(one_window)(starts[0], starts[1])


def lens_shift(previous, target, template):
    shifts = jnp.zeros_like(template)
    for earlier_plane, deflect in enumerate(previous[:target]):
        shifts = shifts - ((target - earlier_plane) / target) * deflect
    return shifts


def plane_step(fine_lookup, long_lookup, fine_cell, long_cell, offsets, shifts):
    fine_x, fine_y = interpolate(fine_lookup, fine_cell[0], fine_cell[1], offsets[0] + shifts[0], offsets[1] + shifts[1])
    long_x, long_y = interpolate(long_lookup, long_cell[0], long_cell[1], offsets[2] + shifts[0] / RATIO, offsets[3] + shifts[1] / RATIO)
    return jnp.stack([fine_x + long_x, fine_y + long_y])


def reference(tile_density, long_maps, map_owner, tile_lists, block_slots, block_windows, fine_cells, long_cells, fractions):
    smooth_table, slope_table = kernel_tables(TS)
    all_fields = jnp.stack([convolve(tile_density[plane_index], smooth_table, slope_table) for plane_index in range(PLANES)])
    used_maps = jnp.stack([lax.dynamic_index_in_dim(long_maps[:, plane_index], map_owner[plane_index], 0, keepdims=False) for plane_index in range(PLANES)])
    groups = N_RAYS * N_PLANES
    blocks = RAYS_DEV // BLK

    def regroup(values):
        return jnp.moveaxis(values.reshape(PLANES, values.shape[1], groups, blocks, BLK), 2, 0)

    slots_grouped = jnp.moveaxis(block_slots.reshape(PLANES, groups, blocks), 1, 0)
    windows_grouped = jnp.moveaxis(block_windows.reshape(PLANES, 2, groups, blocks), 2, 0)

    def trace_group(inputs):
        group_index, slot_ids, window_starts, fine_group, long_group, frac_group = inputs
        bundle_lists = lax.dynamic_index_in_dim(tile_lists, group_index // N_PLANES, 0, keepdims=False)
        deflection_list = []
        for plane_index in range(PLANES):
            tile_ids = jnp.take(bundle_lists[plane_index], slot_ids[plane_index], axis=0)
            fine_lookup = jnp.take(all_fields[plane_index], tile_ids, axis=0)
            long_lookup = map_windows(used_maps[plane_index], window_starts[plane_index], TS)
            template = frac_group[plane_index][:2]
            shifts = lens_shift(deflection_list, plane_index, template)
            deflection_list.append(plane_step(fine_lookup, long_lookup, fine_group[plane_index], long_group[plane_index], frac_group[plane_index], shifts))
        source = lens_shift(deflection_list, PLANES, frac_group[0][:2])
        return jnp.stack(deflection_list), source

    deflect_all, source_all = lax.map(trace_group, (jnp.arange(groups, dtype=jnp.int32), slots_grouped, windows_grouped, regroup(fine_cells), regroup(long_cells), regroup(fractions)))
    deflection = jnp.moveaxis(deflect_all, 0, 2).reshape(PLANES, 2, RAYS)
    source_shift = jnp.moveaxis(source_all, 0, 1).reshape(2, RAYS)
    return deflection, source_shift
```

```python
import jax
import jax.numpy as jnp
from jax import lax
from jax.experimental import pallas as pl
from jax.experimental.pallas import tpu as pltpu
from jax.sharding import PartitionSpec as P

RATIO = 16
BF = jnp.bfloat16
F32 = jnp.float32
SUB = 16
ZG = 4
TAPS = 6


def kernel_tables(side):
    indices = jnp.arange(side, dtype=jnp.int32)
    offset = (indices[:, None] - indices[None, :]).astype(F32)
    tap_offsets = jnp.arange(-TAPS, TAPS + 1, dtype=jnp.int32).astype(F32)
    tap_total = jnp.sum(jnp.exp(-tap_offsets * tap_offsets / 8.0))
    inside = jnp.abs(offset) <= TAPS
    weight = jnp.where(inside, jnp.exp(-offset * offset / 8.0), 0.0) / tap_total
    smooth_table = weight.astype(BF)
    slope_table = (6.0 * offset * weight / 4.0).astype(BF)
    return (smooth_table, slope_table)


def with_next(table):
    following = jnp.concatenate([table[1:], jnp.zeros_like(table[:1])], axis=0)
    return jnp.concatenate([table.T, following.T], axis=1)


def onehot_tiles(row, tiles, width):
    wide = jnp.broadcast_to(row, (SUB, width)).astype(BF)
    place = lax.broadcasted_iota(jnp.int32, (SUB, width), 0).astype(F32)
    one = jnp.ones((SUB, width), BF)
    zero = jnp.zeros((SUB, width), BF)
    return [
        jnp.where(wide == (place + float(SUB * t)).astype(BF), one, zero) for t in range(tiles)
    ]


def corner_sums(parts, columns, select):
    rows, width = parts[0].shape
    tiles = rows // SUB
    here = onehot_tiles(columns, tiles, width)
    after = onehot_tiles(columns + 1.0, tiles, width)
    sums = []
    for part in parts:
        low = part.astype(BF)
        for hot in (here, after):
            total = low[:SUB] * hot[0]
            for t in range(1, tiles):
                total = total + low[t * SUB : (t + 1) * SUB] * hot[t]
            sums.append(total)
    stacked = jnp.concatenate(sums, axis=0)
    return jnp.dot(select, stacked, preferred_element_type=F32)[:8]


def fine_kernel(slot_ref, entry_ref, tiles_ref, cells_ref, left_ref, slope_ref, smooth_ref, select_ref, out_ref):
    step = pl.program_id(0)
    width = 512
    per_step = out_ref.shape[2] // width
    side = tiles_ref.shape[2]
    for b in range(per_step):
        slot = entry_ref[slot_ref[step * per_step + b]]
        density = tiles_ref[slot]
        lanes = slice(b * width, (b + 1) * width)
        partial = lax.dot_general(
            left_ref[...], density, (((1,), (1,)), ((), ())), preferred_element_type=F32
        ).astype(BF)
        along_x = jnp.dot(partial[:side], slope_ref[...], preferred_element_type=F32).astype(BF)
        along_y = jnp.dot(partial[side:], smooth_ref[...], preferred_element_type=F32).astype(BF)
        table = jnp.concatenate(
            [along_x[:, :side], along_y[:, :side], along_x[:, side:], along_y[:, side:]], axis=0
        )
        hot = jnp.concatenate(onehot_tiles(cells_ref[0, 0:1, lanes], side // SUB, width), axis=0)
        found = jnp.dot(table, hot, preferred_element_type=F32)
        parts = [found[i * side : (i + 1) * side] for i in range(4)]
        corners = corner_sums(parts, cells_ref[0, 1:2, lanes], select_ref[...])
        out_ref[0, :, lanes] = corners.astype(BF)


def long_kernel(start_ref, map_ref, next_ref, cells_ref, select_ref, out_ref):
    step = pl.program_id(0)
    width = 512
    per_step = out_ref.shape[2] // width
    extent = map_ref.shape[1]
    side = 128
    rows = side + SUB
    for b in range(per_step):
        block = step * per_step + b
        row_start = start_ref[0, block]
        col_start = start_ref[1, block]
        row_base = jnp.minimum(row_start // side, extent // side - 2) * side
        col_base = jnp.minimum(col_start // SUB, (extent - rows) // SUB) * SUB
        row_base = pl.multiple_of(row_base, side)
        col_base = pl.multiple_of(col_base, SUB)
        lanes = slice(b * width, (b + 1) * width)
        take = (pl.ds(col_base, rows), pl.ds(row_base, 2 * side))
        table = jnp.concatenate(
            [map_ref[(0, *take)], map_ref[(1, *take)], next_ref[(0, *take)], next_ref[(1, *take)]],
            axis=0,
        )
        row = cells_ref[0, 2:3, lanes] + (row_start - row_base).astype(F32)
        col = cells_ref[0, 3:4, lanes] + (col_start - col_base).astype(F32)
        hot = jnp.concatenate(onehot_tiles(row, 2 * side // SUB, width), axis=0)
        found = jnp.dot(table, hot, preferred_element_type=F32)
        parts = [found[i * rows : (i + 1) * rows] for i in range(4)]
        out_ref[0, :, lanes] = corner_sums(parts, col, select_ref[...]).astype(BF)


def table_value(corners, p, q):
    rw0 = (1.0 - p).astype(BF).astype(F32)
    rw1 = p.astype(BF).astype(F32)
    cw0, cw1 = 1.0 - q, q
    v = [corners[i : i + 1] for i in range(8)]
    along_x = (rw0 * v[0] + rw1 * v[4]) * cw0 + (rw0 * v[1] + rw1 * v[5]) * cw1
    along_y = (rw0 * v[2] + rw1 * v[6]) * cw0 + (rw0 * v[3] + rw1 * v[7]) * cw1
    return along_x, along_y


def lens_shift(previous, target):
    shift_x, shift_y = 0.0, 0.0
    for earlier, (x, y) in enumerate(previous):
        factor = (target - earlier) / target
        shift_x, shift_y = shift_x - factor * x, shift_y - factor * y
    return shift_x, shift_y


def final_kernel(fine_ref, long_ref, frac_ref, deflection_ref, source_ref):
    planes = fine_ref.shape[0]
    found = []
    for k in range(planes):
        frac = frac_ref[k]
        sx, sy = lens_shift(found, k)
        fx, fy = table_value(fine_ref[k].astype(F32), frac[0:1] + sx, frac[1:2] + sy)
        lx, ly = table_value(
            long_ref[k].astype(F32), frac[2:3] + sx / RATIO, frac[3:4] + sy / RATIO
        )
        found.append((fx + lx, fy + ly))
        deflection_ref[k, 0:1] = found[k][0]
        deflection_ref[k, 1:2] = found[k][1]
    sx, sy = lens_shift(found, planes)
    source_ref[0:1] = sx
    source_ref[1:2] = sy


def per_device(
    tile_density,
    long_maps,
    map_owner,
    tile_lists,
    block_slots,
    block_windows,
    fine_cells,
    long_cells,
    fractions,
):
    my_row = lax.axis_index("rays")
    plane = lax.axis_index("planes")
    planes, tile_dev, strip, side = tile_density.shape
    extent = long_maps.shape[2]
    list_len = tile_lists.shape[2]
    rays_here = fine_cells.shape[2]
    blocks = block_slots.shape[1]
    ray_count = lax.axis_size("rays")
    level = ray_count // ZG
    my_z, my_xy = my_row // level, my_row % level
    flat_groups = [[z * level + i for i in range(level)] for z in range(ZG)]

    def along_z(x, d):
        pairs = [(r, (r // level + d) % ZG * level + r % level) for r in range(ray_count)]
        return lax.ppermute(x, "rays", pairs)

    def exchange_flat(x):
        return lax.all_to_all(x, "rays", 0, 0, tiled=True, axis_index_groups=flat_groups)

    small = jnp.concatenate(
        [
            block_slots[:, None, :],
            block_windows // SUB,
            block_windows % SUB,
        ],
        axis=1,
    ).reshape(planes, 1, 5 * blocks)
    small = jnp.pad(small, ((0, 0), (0, 3), (0, 128 - 5 * blocks)))
    cells = jnp.concatenate([fine_cells, long_cells], axis=1)
    ray_info = jnp.concatenate([cells, small], axis=2).astype(BF)
    ray_info = lax.all_to_all(ray_info, "planes", 0, 0, tiled=True)
    cells = ray_info[:, :, :rays_here].astype(F32)
    small = ray_info[:, 0, rays_here : rays_here + 5 * blocks].astype(jnp.int32)
    small = small.reshape(planes, 5, blocks)
    slots = small[:, 0].reshape(planes * blocks)
    starts = (small[:, 1:3] * SUB + small[:, 3:5]).transpose(1, 0, 2).reshape(2, planes * blocks)

    tiles = lax.all_to_all(tile_density, "planes", 0, 0, tiled=True)
    tiles = tiles.transpose(1, 0, 2, 3).reshape(tile_dev, side, side)
    column = jnp.stack([tiles] + [along_z(tiles, d) for d in range(1, ZG)])
    level_lists = lax.dynamic_slice(tile_lists, (my_z * level, plane, 0), (level, 1, list_len))[:, 0]
    owners = level_lists // tile_dev
    key = jnp.arange(list_len, dtype=jnp.int32) * tile_dev + level_lists % tile_dev
    column_owner = (my_z - jnp.arange(ZG, dtype=jnp.int32)) % ZG * level + my_xy
    mine = owners[:, None, :] == column_owner[None, :, None]
    first = jnp.min(jnp.where(mine, key[:, None, :], tile_dev * list_len), axis=2) % tile_dev
    last = jnp.max(jnp.where(mine, key[:, None, :], 0), axis=2) % tile_dev
    wanted = jnp.stack([first, last], axis=2)[:, :, :, None, None]
    outgoing = jnp.broadcast_to(column[None, :, None, 0], (level, ZG, 2, side, side))
    for t in range(1, tile_dev):
        outgoing = jnp.where(wanted == t, column[None, :, None, t], outgoing)
    incoming = exchange_flat(outgoing).reshape(level * ZG * 2, side, side)

    my_list = lax.dynamic_slice(tile_lists, (my_row, plane, 0), (1, 1, list_len))[0, 0]
    my_owner = my_list // tile_dev
    place = jnp.arange(list_len, dtype=jnp.int32)
    repeat = (my_owner[:, None] == my_owner[None, :]) & (place[:, None] > place[None, :])
    rank = jnp.max(repeat.astype(jnp.int32), axis=1)
    entry = my_owner % level * (2 * ZG) + (my_z - my_owner // level) % ZG * 2 + rank

    own_map = lax.dynamic_index_in_dim(long_maps[0], plane, 0, keepdims=False)
    own_map = own_map.transpose(1, 2, 0).reshape(level, 2 * extent // level, extent)
    owner = lax.dynamic_index_in_dim(map_owner, plane, 0, keepdims=False)
    pieces = exchange_flat(own_map)
    piece = lax.dynamic_index_in_dim(pieces, owner % level, 0, keepdims=False)
    distance = (my_z - owner // level) % ZG
    chosen = piece
    for d in range(1, ZG):
        chosen = jnp.where(distance == d, along_z(piece, d), chosen)
    whole = exchange_flat(jnp.broadcast_to(chosen[None], (level, *chosen.shape)))
    whole = whole.reshape(2, extent, extent)
    following = jnp.concatenate([whole[:, :, 1:], whole[:, :, :1]], axis=2)

    select = (jnp.arange(8 * SUB)[None, :] // SUB == jnp.arange(SUB)[:, None]).astype(BF)
    smooth_table, slope_table = kernel_tables(side)
    left = jnp.concatenate([smooth_table, slope_table], axis=0)
    wide = 2048
    per_plane = rays_here // wide
    vmem = pl.BlockSpec(memory_space=pltpu.VMEM)
    cell_spec = pl.BlockSpec((1, 4, wide), lambda g, *_: (g // per_plane, 0, g % per_plane))
    out_spec = pl.BlockSpec((1, 8, wide), lambda g, *_: (g // per_plane, 0, g % per_plane))
    corner_shape = jax.ShapeDtypeStruct((planes, 8, rays_here), BF)
    params = pltpu.CompilerParams(vmem_limit_bytes=48 << 20)
    long_corners = pl.pallas_call(
        long_kernel,
        out_shape=corner_shape,
        grid_spec=pltpu.PrefetchScalarGridSpec(
            num_scalar_prefetch=1,
            grid=(planes * per_plane,),
            in_specs=[vmem, vmem, cell_spec, vmem],
            out_specs=out_spec,
        ),
        compiler_params=params,
        name="long_gather",
    )(starts, whole, following, cells, select)
    long_corners = lax.all_to_all(long_corners, "planes", 0, 0, tiled=True)
    fine_corners = pl.pallas_call(
        fine_kernel,
        out_shape=corner_shape,
        grid_spec=pltpu.PrefetchScalarGridSpec(
            num_scalar_prefetch=2,
            grid=(planes * per_plane,),
            in_specs=[vmem, cell_spec, vmem, vmem, vmem, vmem],
            out_specs=out_spec,
        ),
        compiler_params=params,
        name="fine_gather",
    )(slots, entry, incoming, cells, left, with_next(slope_table), with_next(smooth_table), select)
    fine_corners = lax.all_to_all(fine_corners, "planes", 0, 0, tiled=True)

    return pl.pallas_call(
        final_kernel,
        out_shape=(
            jax.ShapeDtypeStruct((planes, 2, rays_here), F32),
            jax.ShapeDtypeStruct((2, rays_here), F32),
        ),
        grid=(per_plane,),
        in_specs=[
            pl.BlockSpec((planes, 8, wide), lambda g: (0, 0, g)),
            pl.BlockSpec((planes, 8, wide), lambda g: (0, 0, g)),
            pl.BlockSpec((planes, 4, wide), lambda g: (0, 0, g)),
        ],
        out_specs=(
            pl.BlockSpec((planes, 2, wide), lambda g: (0, 0, g)),
            pl.BlockSpec((2, wide), lambda g: (0, g)),
        ),
        name="lens_sum",
    )(fine_corners, long_corners, fractions)


def solution(mesh):
    return jax.shard_map(
        per_device,
        mesh=mesh,
        in_specs=(
            P(None, "rays", "planes", None),
            P("rays", None, None, None, None),
            P(),
            P(),
            P(None, ("rays", "planes")),
            P(None, None, ("rays", "planes")),
            P(None, None, ("rays", "planes")),
            P(None, None, ("rays", "planes")),
            P(None, None, ("rays", "planes")),
        ),
        out_specs=(P(None, None, ("rays", "planes")), P(None, ("rays", "planes"))),
        check_vma=False,
    )
```

```python
import jax
import jax.numpy as jnp
from jax import lax
from jax.experimental import pallas as pl
from jax.experimental.pallas import tpu as pltpu
from jax.sharding import PartitionSpec as P

RATIO = 16
BF = jnp.bfloat16
F32 = jnp.float32
SUB = 16
ZG = 4
TAPS = 6


def kernel_tables(side):
    indices = jnp.arange(side, dtype=jnp.int32)
    offset = (indices[:, None] - indices[None, :]).astype(F32)
    tap_offsets = jnp.arange(-TAPS, TAPS + 1, dtype=jnp.int32).astype(F32)
    tap_total = jnp.sum(jnp.exp(-tap_offsets * tap_offsets / 8.0))
    inside = jnp.abs(offset) <= TAPS
    weight = jnp.where(inside, jnp.exp(-offset * offset / 8.0), 0.0) / tap_total
    smooth_table = weight.astype(BF)
    slope_table = (6.0 * offset * weight / 4.0).astype(BF)
    return (smooth_table, slope_table)


def with_next(table):
    following = jnp.concatenate([table[1:], jnp.zeros_like(table[:1])], axis=0)
    return jnp.concatenate([table.T, following.T], axis=1)


def onehot_tiles(row, tiles, width):
    wide = jnp.broadcast_to(row, (SUB, width)).astype(BF)
    place = lax.broadcasted_iota(jnp.int32, (SUB, width), 0).astype(F32)
    one = jnp.ones((SUB, width), BF)
    zero = jnp.zeros((SUB, width), BF)
    return [
        jnp.where(wide == (place + float(SUB * t)).astype(BF), one, zero) for t in range(tiles)
    ]


def corner_sums(found, columns, select):
    rows = found.shape[0] // 4
    half = found.shape[1] // 2
    results = []
    for h in range(2):
        lanes = slice(h * half, (h + 1) * half)
        column = columns[:, lanes]
        tile_of = [jnp.floor((column + step) * (1.0 / SUB)) for step in (0.0, 1.0)]
        wide = [jnp.broadcast_to(t, (SUB, half)).astype(BF) for t in tile_of]
        kept = [[None, None] for _ in range(4)]
        for t in range(rows // SUB):
            hit = [w == float(t) for w in wide]
            for i in range(4):
                low = found[i * rows + t * SUB : i * rows + (t + 1) * SUB, lanes].astype(BF)
                for s in range(2):
                    kept[i][s] = low if t == 0 else jnp.where(hit[s], low, kept[i][s])
        hot = [onehot_tiles(column + s - SUB * tile_of[s], 1, half)[0] for s in range(2)]
        stacked = jnp.concatenate([kept[i][s] * hot[s] for i in range(4) for s in range(2)], axis=0)
        results.append(jnp.dot(select, stacked, preferred_element_type=F32)[:8])
    return jnp.concatenate(results, axis=1)


def pipelined(count, stages):
    held = {}
    for turn in range(count + len(stages) - 1):
        for s, stage in enumerate(stages):
            item = turn - s
            if 0 <= item < count:
                held[item] = stage(item, held.get(item))


def fine_kernel(whose_ref, slot_ref, entry_ref, tiles_ref, cells_ref, left_ref, slope_ref, smooth_ref, select_ref, out_ref):
    step = pl.program_id(0)
    width = 512
    per_step = out_ref.shape[2] // width
    places, strips = tiles_ref.shape[1:3]
    side = tiles_ref.shape[4]

    def lanes(b):
        return slice(b * width, (b + 1) * width)

    def columns_done(b, _):
        entry = entry_ref[slot_ref[step * per_step + b]]
        source, place = entry // strips, entry % strips
        density = jnp.concatenate([tiles_ref[source, i, place] for i in range(places)], axis=0)
        return lax.dot_general(
            left_ref[...], density, (((1,), (1,)), ((), ())), preferred_element_type=F32
        ).astype(BF)

    def fields(b, partial):
        along_x = jnp.dot(partial[:side], slope_ref[...], preferred_element_type=F32).astype(BF)
        along_y = jnp.dot(partial[side:], smooth_ref[...], preferred_element_type=F32).astype(BF)
        return jnp.concatenate(
            [along_x[:, :side], along_y[:, :side], along_x[:, side:], along_y[:, side:]], axis=0
        )

    def gather_rows(b, table):
        hot = jnp.concatenate(onehot_tiles(cells_ref[0, 0:1, lanes(b)], side // SUB, width), axis=0)
        return jnp.dot(table, hot, preferred_element_type=F32)

    def gather_columns(b, found):
        corners = corner_sums(found, cells_ref[0, 1:2, lanes(b)], select_ref[...])
        out_ref[0, :, lanes(b)] = corners.astype(BF)

    pipelined(per_step, (columns_done, fields, gather_rows, gather_columns))


def long_kernel(whose_ref, start_ref, map_ref, cells_ref, select_ref, out_ref):
    step = pl.program_id(0)
    width = 512
    per_step = out_ref.shape[2] // width
    extent = map_ref.shape[1]
    side = 128
    rows = side + SUB

    def lanes(b):
        return slice(b * width, (b + 1) * width)

    def bases(b):
        row_start = start_ref[0, step * per_step + b]
        col_start = start_ref[1, step * per_step + b]
        row_base = jnp.minimum(row_start // side, extent // side - 2) * side
        col_base = jnp.minimum(col_start // SUB, (extent - rows) // SUB) * SUB
        return row_start, pl.multiple_of(row_base, side), col_start, pl.multiple_of(col_base, SUB)

    def gather_rows(b, _):
        row_start, row_base, _, col_base = bases(b)
        take = (pl.ds(col_base, rows), pl.ds(row_base, 2 * side))
        table = jnp.concatenate([map_ref[(0, *take)], map_ref[(1, *take)]], axis=0)
        table = jnp.concatenate([table, pltpu.roll(table, 2 * side - 1, axis=1)], axis=0)
        row = cells_ref[0, 2:3, lanes(b)] + (row_start - row_base).astype(F32)
        hot = jnp.concatenate(onehot_tiles(row, 2 * side // SUB, width), axis=0)
        return jnp.dot(table, hot, preferred_element_type=F32)

    def gather_columns(b, found):
        _, _, col_start, col_base = bases(b)
        col = cells_ref[0, 3:4, lanes(b)] + (col_start - col_base).astype(F32)
        out_ref[0, :, lanes(b)] = corner_sums(found, col, select_ref[...]).astype(BF)

    pipelined(per_step, (gather_rows, gather_columns))


def table_value(corners, p, q):
    rw0 = (1.0 - p).astype(BF).astype(F32)
    rw1 = p.astype(BF).astype(F32)
    cw0, cw1 = 1.0 - q, q
    v = [corners[i : i + 1] for i in range(8)]
    along_x = (rw0 * v[0] + rw1 * v[4]) * cw0 + (rw0 * v[1] + rw1 * v[5]) * cw1
    along_y = (rw0 * v[2] + rw1 * v[6]) * cw0 + (rw0 * v[3] + rw1 * v[7]) * cw1
    return along_x, along_y


def lens_shift(previous, target):
    shift_x, shift_y = 0.0, 0.0
    for earlier, (x, y) in enumerate(previous):
        factor = (target - earlier) / target
        shift_x, shift_y = shift_x - factor * x, shift_y - factor * y
    return shift_x, shift_y


def final_kernel(fine_ref, long_ref, frac_ref, deflection_ref, source_ref):
    planes = fine_ref.shape[0]
    found = []
    for k in range(planes):
        frac = frac_ref[k]
        sx, sy = lens_shift(found, k)
        fx, fy = table_value(fine_ref[k].astype(F32), frac[0:1] + sx, frac[1:2] + sy)
        lx, ly = table_value(
            long_ref[k].astype(F32), frac[2:3] + sx / RATIO, frac[3:4] + sy / RATIO
        )
        found.append((fx + lx, fy + ly))
        deflection_ref[k, 0:1] = found[k][0]
        deflection_ref[k, 1:2] = found[k][1]
    sx, sy = lens_shift(found, planes)
    source_ref[0:1] = sx
    source_ref[1:2] = sy


def per_device(
    tile_density,
    long_maps,
    map_owner,
    tile_lists,
    block_slots,
    block_windows,
    fine_cells,
    long_cells,
    fractions,
):
    my_row = lax.axis_index("rays")
    plane = lax.axis_index("planes")
    planes, tile_dev, strip, side = tile_density.shape
    extent = long_maps.shape[2]
    list_len = tile_lists.shape[2]
    rays_here = fine_cells.shape[2]
    blocks = block_slots.shape[1]
    ray_count = lax.axis_size("rays")
    level = ray_count // ZG
    my_z, my_xy = my_row // level, my_row % level
    flat_groups = [[z * level + i for i in range(level)] for z in range(ZG)]

    def along_z(x, d):
        pairs = [(r, (r // level + d) % ZG * level + r % level) for r in range(ray_count)]
        return lax.ppermute(x, "rays", pairs)

    def exchange_flat(x):
        return lax.all_to_all(x, "rays", 0, 0, tiled=True, axis_index_groups=flat_groups)

    column = jnp.stack([tile_density] + [along_z(tile_density, d) for d in range(1, ZG)])

    own_map = lax.dynamic_index_in_dim(long_maps[0], plane, 0, keepdims=False)
    own_map = own_map.transpose(1, 2, 0).reshape(level, 2 * extent // level, extent)
    owner = lax.dynamic_index_in_dim(map_owner, plane, 0, keepdims=False)
    pieces = exchange_flat(own_map)
    piece = lax.dynamic_index_in_dim(pieces, owner % level, 0, keepdims=False)

    level_lists = lax.dynamic_slice(tile_lists, (my_z * level, 0, 0), (level, planes, list_len))
    owners = level_lists // tile_dev
    key = jnp.arange(list_len, dtype=jnp.int32) * tile_dev + level_lists % tile_dev
    column_owner = (my_z - jnp.arange(ZG, dtype=jnp.int32)) % ZG * level + my_xy
    mine = owners[:, :, None, :] == column_owner[None, None, :, None]
    first = jnp.min(jnp.where(mine, key[:, :, None, :], tile_dev * list_len), axis=3) % tile_dev
    last = jnp.max(jnp.where(mine, key[:, :, None, :], 0), axis=3) % tile_dev
    wanted = jnp.stack([first, last], axis=3)[..., None, None]
    by_plane = column.transpose(1, 0, 2, 3, 4)
    outgoing = jnp.broadcast_to(
        by_plane[None, :, :, None, 0], (level, planes, ZG, 2, strip, side)
    )
    for t in range(1, tile_dev):
        outgoing = jnp.where(wanted == t, by_plane[None, :, :, None, t], outgoing)
    outgoing, piece = lax.optimization_barrier((outgoing, piece))
    incoming = lax.all_to_all(
        outgoing.reshape(level * planes, ZG * 2, strip, side),
        ("rays", "planes"),
        0,
        0,
        tiled=True,
        axis_index_groups=[
            list(range(z * level * planes, (z + 1) * level * planes)) for z in range(ZG)
        ],
    ).reshape(level, planes, ZG * 2, strip, side)

    distance = (my_z - owner // level) % ZG
    chosen = piece
    for d in range(1, ZG):
        chosen = jnp.where(distance == d, along_z(piece, d), chosen)

    my_list = lax.dynamic_slice(tile_lists, (my_row, plane, 0), (1, 1, list_len))[0, 0]
    my_owner = my_list // tile_dev
    place = jnp.arange(list_len, dtype=jnp.int32)
    repeat = (my_owner[:, None] == my_owner[None, :]) & (place[:, None] > place[None, :])
    rank = jnp.max(repeat.astype(jnp.int32), axis=1)
    entry = my_owner % level * (2 * ZG) + (my_z - my_owner // level) % ZG * 2 + rank

    block_slots, block_windows, fine_cells, long_cells, _ = lax.optimization_barrier(
        (block_slots, block_windows, fine_cells, long_cells, column[ZG - 1, 0, 0, 0, :1])
    )
    small = jnp.concatenate(
        [block_slots[:, None, :], block_windows // SUB, block_windows % SUB], axis=1
    ).reshape(planes, 1, 5 * blocks)
    small = jnp.pad(small, ((0, 0), (0, 3), (0, 128 - 5 * blocks)))
    cells = jnp.concatenate([fine_cells, long_cells], axis=1)
    ray_info = jnp.concatenate([cells, small], axis=2).astype(BF)
    arrived = [lax.dynamic_index_in_dim(ray_info, plane, 0, keepdims=False)]
    for d in range(1, planes):
        pairs = [(i, (i + d) % planes) for i in range(planes)]
        sent = lax.dynamic_index_in_dim(ray_info, (plane + d) % planes, 0, keepdims=False)
        arrived.append(lax.ppermute(sent, "planes", pairs))
    arrived = jnp.stack(arrived)
    cells = arrived[:, :, :rays_here].astype(F32)
    small = arrived[:, 0, rays_here : rays_here + 5 * blocks].astype(jnp.int32)
    small = small.reshape(planes, 5, blocks)
    turn = (plane - jnp.arange(planes)) % planes
    small = jnp.sum(
        jnp.where(turn[:, None] == jnp.arange(planes), 1, 0)[:, :, None, None] * small[None], axis=1
    )
    slots = small[:, 0].reshape(planes * blocks)
    starts = (small[:, 1:3] * SUB + small[:, 3:5]).transpose(1, 0, 2).reshape(2, planes * blocks)
    whose = plane.reshape(1)

    chosen, incoming = lax.optimization_barrier((chosen, incoming))
    whole = exchange_flat(jnp.broadcast_to(chosen[None], (level, *chosen.shape)))
    whole = whole.reshape(2, extent, extent)

    select = (jnp.arange(8 * SUB)[None, :] // SUB == jnp.arange(SUB)[:, None]).astype(BF)
    smooth_table, slope_table = kernel_tables(side)
    left = jnp.concatenate([smooth_table, slope_table], axis=0)
    wide = 4096
    per_plane = rays_here // wide
    vmem = pl.BlockSpec(memory_space=pltpu.VMEM)
    cell_spec = pl.BlockSpec(
        (1, 4, wide),
        lambda g, whose, *_: ((whose[0] + planes - g // per_plane) % planes, 0, g % per_plane),
    )
    out_spec = pl.BlockSpec((1, 8, wide), lambda g, *_: (g // per_plane, 0, g % per_plane))
    corner_shape = jax.ShapeDtypeStruct((planes, 8, rays_here), BF)
    params = pltpu.CompilerParams(vmem_limit_bytes=48 << 20)
    fine_corners = pl.pallas_call(
        fine_kernel,
        out_shape=corner_shape,
        grid_spec=pltpu.PrefetchScalarGridSpec(
            num_scalar_prefetch=3,
            grid=(planes * per_plane,),
            in_specs=[vmem, cell_spec, vmem, vmem, vmem, vmem],
            out_specs=out_spec,
        ),
        compiler_params=params,
        name="fine_gather",
    )(whose, slots, entry, incoming, cells, left, with_next(slope_table), with_next(smooth_table), select)
    fine_corners, whole = lax.optimization_barrier((fine_corners, whole))
    fine_corners = lax.all_to_all(fine_corners, "planes", 0, 0, tiled=True)
    long_corners = pl.pallas_call(
        long_kernel,
        out_shape=corner_shape,
        grid_spec=pltpu.PrefetchScalarGridSpec(
            num_scalar_prefetch=2,
            grid=(planes * per_plane,),
            in_specs=[vmem, cell_spec, vmem],
            out_specs=out_spec,
        ),
        compiler_params=params,
        name="long_gather",
    )(whose, starts, whole, cells, select)
    long_corners, fine_corners = lax.optimization_barrier((long_corners, fine_corners))
    long_corners = lax.all_to_all(long_corners, "planes", 0, 0, tiled=True)
    wide = 2048

    return pl.pallas_call(
        final_kernel,
        out_shape=(
            jax.ShapeDtypeStruct((planes, 2, rays_here), F32),
            jax.ShapeDtypeStruct((2, rays_here), F32),
        ),
        grid=(rays_here // wide,),
        in_specs=[
            pl.BlockSpec((planes, 8, wide), lambda g: (0, 0, g)),
            pl.BlockSpec((planes, 8, wide), lambda g: (0, 0, g)),
            pl.BlockSpec((planes, 4, wide), lambda g: (0, 0, g)),
        ],
        out_specs=(
            pl.BlockSpec((planes, 2, wide), lambda g: (0, 0, g)),
            pl.BlockSpec((2, wide), lambda g: (0, g)),
        ),
        name="lens_sum",
    )(fine_corners, long_corners, fractions)


def solution(mesh):
    return jax.shard_map(
        per_device,
        mesh=mesh,
        in_specs=(
            P(None, "rays", "planes", None),
            P("rays", None, None, None, None),
            P(),
            P(),
            P(None, ("rays", "planes")),
            P(None, None, ("rays", "planes")),
            P(None, None, ("rays", "planes")),
            P(None, None, ("rays", "planes")),
            P(None, None, ("rays", "planes")),
        ),
        out_specs=(P(None, None, ("rays", "planes")), P(None, ("rays", "planes"))),
        check_vma=False,
    )
```

```python
import functools

import jax
import jax.numpy as jnp
from jax import lax
from jax.experimental import pallas as pl
from jax.experimental.pallas import tpu as pltpu
from jax.sharding import PartitionSpec as P

RATIO = 16
BF = jnp.bfloat16
F32 = jnp.float32
SUB = 16
ZG = 4
TAPS = 6


def kernel_tables(side):
    indices = jnp.arange(side, dtype=jnp.int32)
    offset = (indices[:, None] - indices[None, :]).astype(F32)
    tap_offsets = jnp.arange(-TAPS, TAPS + 1, dtype=jnp.int32).astype(F32)
    tap_total = jnp.sum(jnp.exp(-tap_offsets * tap_offsets / 8.0))
    inside = jnp.abs(offset) <= TAPS
    weight = jnp.where(inside, jnp.exp(-offset * offset / 8.0), 0.0) / tap_total
    smooth_table = weight.astype(BF)
    slope_table = (6.0 * offset * weight / 4.0).astype(BF)
    return (smooth_table, slope_table)


def with_next(table):
    following = jnp.concatenate([table[1:], jnp.zeros_like(table[:1])], axis=0)
    return jnp.concatenate([table.T, following.T], axis=1)


def onehot_tiles(row, tiles, width):
    wide = jnp.broadcast_to(row, (SUB, width)).astype(BF)
    place = lax.broadcasted_iota(jnp.int32, (SUB, width), 0).astype(F32)
    one = jnp.ones((SUB, width), BF)
    zero = jnp.zeros((SUB, width), BF)
    return [
        jnp.where(wide == (place + float(SUB * t)).astype(BF), one, zero) for t in range(tiles)
    ]


def corner_sums(found, columns, select):
    rows = found.shape[0] // 4
    half = found.shape[1] // 2
    results = []
    for h in range(2):
        lanes = slice(h * half, (h + 1) * half)
        column = columns[:, lanes]
        tile_of = [jnp.floor((column + step) * (1.0 / SUB)) for step in (0.0, 1.0)]
        wide = [jnp.broadcast_to(t, (SUB, half)).astype(BF) for t in tile_of]
        kept = [[None, None] for _ in range(4)]
        for t in range(rows // SUB):
            hit = [w == float(t) for w in wide]
            for i in range(4):
                low = found[i * rows + t * SUB : i * rows + (t + 1) * SUB, lanes].astype(BF)
                for s in range(2):
                    kept[i][s] = low if t == 0 else jnp.where(hit[s], low, kept[i][s])
        hot = [onehot_tiles(column + s - SUB * tile_of[s], 1, half)[0] for s in range(2)]
        stacked = jnp.concatenate([kept[i][s] * hot[s] for i in range(4) for s in range(2)], axis=0)
        results.append(jnp.dot(select, stacked, preferred_element_type=F32)[:8])
    return jnp.concatenate(results, axis=1)


def pipelined(count, stages):
    held = {}
    for turn in range(count + len(stages) - 1):
        for s, stage in enumerate(stages):
            item = turn - s
            if 0 <= item < count:
                held[item] = stage(item, held.get(item))


def fine_kernel(part, parts, whose_ref, slot_ref, entry_ref, tiles_ref, cells_ref, left_ref, slope_ref, smooth_ref, select_ref, out_ref):
    step = pl.program_id(0)
    width = 512
    per_step = out_ref.shape[2] // width
    places, strips = tiles_ref.shape[1:3]
    side = tiles_ref.shape[4]

    def lanes(b):
        return slice(b * width, (b + 1) * width)

    def columns_done(b, _):
        entry = entry_ref[slot_ref[(step * parts + part) * per_step + b]]
        source, place = entry // strips, entry % strips
        density = jnp.concatenate([tiles_ref[source, i, place] for i in range(places)], axis=0)
        return lax.dot_general(
            left_ref[...], density, (((1,), (1,)), ((), ())), preferred_element_type=F32
        ).astype(BF)

    def fields(b, partial):
        along_x = jnp.dot(partial[:side], slope_ref[...], preferred_element_type=F32).astype(BF)
        along_y = jnp.dot(partial[side:], smooth_ref[...], preferred_element_type=F32).astype(BF)
        return jnp.concatenate(
            [along_x[:, :side], along_y[:, :side], along_x[:, side:], along_y[:, side:]], axis=0
        )

    def gather_rows(b, table):
        hot = jnp.concatenate(onehot_tiles(cells_ref[0, 0:1, lanes(b)], side // SUB, width), axis=0)
        return jnp.dot(table, hot, preferred_element_type=F32)

    def gather_columns(b, found):
        corners = corner_sums(found, cells_ref[0, 1:2, lanes(b)], select_ref[...])
        out_ref[0, :, lanes(b)] = corners.astype(BF)

    pipelined(per_step, (columns_done, fields, gather_rows, gather_columns))


def long_kernel(whose_ref, start_ref, map_ref, cells_ref, select_ref, out_ref):
    step = pl.program_id(0)
    width = 512
    per_step = out_ref.shape[2] // width
    extent = map_ref.shape[1]
    side = 128
    rows = side + SUB

    def lanes(b):
        return slice(b * width, (b + 1) * width)

    def bases(b):
        row_start = start_ref[0, step * per_step + b]
        col_start = start_ref[1, step * per_step + b]
        row_base = jnp.minimum(row_start // side, extent // side - 2) * side
        col_base = jnp.minimum(col_start // SUB, (extent - rows) // SUB) * SUB
        return row_start, pl.multiple_of(row_base, side), col_start, pl.multiple_of(col_base, SUB)

    def gather_rows(b, _):
        row_start, row_base, _, col_base = bases(b)
        take = (pl.ds(col_base, rows), pl.ds(row_base, 2 * side))
        table = jnp.concatenate([map_ref[(0, *take)], map_ref[(1, *take)]], axis=0)
        table = jnp.concatenate([table, pltpu.roll(table, 2 * side - 1, axis=1)], axis=0)
        row = cells_ref[0, 2:3, lanes(b)] + (row_start - row_base).astype(F32)
        hot = jnp.concatenate(onehot_tiles(row, 2 * side // SUB, width), axis=0)
        return jnp.dot(table, hot, preferred_element_type=F32)

    def gather_columns(b, found):
        _, _, col_start, col_base = bases(b)
        col = cells_ref[0, 3:4, lanes(b)] + (col_start - col_base).astype(F32)
        out_ref[0, :, lanes(b)] = corner_sums(found, col, select_ref[...]).astype(BF)

    pipelined(per_step, (gather_rows, gather_columns))


def table_value(corners, p, q):
    rw0 = (1.0 - p).astype(BF).astype(F32)
    rw1 = p.astype(BF).astype(F32)
    cw0, cw1 = 1.0 - q, q
    v = [corners[i : i + 1] for i in range(8)]
    along_x = (rw0 * v[0] + rw1 * v[4]) * cw0 + (rw0 * v[1] + rw1 * v[5]) * cw1
    along_y = (rw0 * v[2] + rw1 * v[6]) * cw0 + (rw0 * v[3] + rw1 * v[7]) * cw1
    return along_x, along_y


def lens_shift(previous, target):
    shift_x, shift_y = 0.0, 0.0
    for earlier, (x, y) in enumerate(previous):
        factor = (target - earlier) / target
        shift_x, shift_y = shift_x - factor * x, shift_y - factor * y
    return shift_x, shift_y


def final_kernel(held, fine_ref, long_ref, frac_ref, *refs):
    deflection_ref, source_ref = refs[held:]
    planes = fine_ref.shape[0]
    found = []
    for k in range(planes):
        frac = frac_ref[k]
        sx, sy = lens_shift(found, k)
        fx, fy = table_value(fine_ref[k].astype(F32), frac[0:1] + sx, frac[1:2] + sy)
        lx, ly = table_value(
            long_ref[k].astype(F32), frac[2:3] + sx / RATIO, frac[3:4] + sy / RATIO
        )
        found.append((fx + lx, fy + ly))
        deflection_ref[k, 0:1] = found[k][0]
        deflection_ref[k, 1:2] = found[k][1]
    sx, sy = lens_shift(found, planes)
    source_ref[0:1] = sx
    source_ref[1:2] = sy


def per_device(
    tile_density,
    long_maps,
    map_owner,
    tile_lists,
    block_slots,
    block_windows,
    fine_cells,
    long_cells,
    fractions,
):
    my_row = lax.axis_index("rays")
    plane = lax.axis_index("planes")
    planes, tile_dev, strip, side = tile_density.shape
    extent = long_maps.shape[2]
    list_len = tile_lists.shape[2]
    rays_here = fine_cells.shape[2]
    blocks = block_slots.shape[1]
    ray_count = lax.axis_size("rays")
    level = ray_count // ZG
    my_z, my_xy = my_row // level, my_row % level
    flat_groups = [[z * level + i for i in range(level)] for z in range(ZG)]

    def moved(x, stride, d):
        pairs = [(r, r + ((r // stride + d) % ZG - r // stride % ZG) * stride) for r in range(ray_count)]
        return lax.ppermute(x, "rays", pairs)

    def along_z(x, d):
        return moved(x, level, d)

    def gathered(x, stride):
        ring = [moved(x, stride, d) for d in range(ZG - 1, 0, -1)] + [x]
        first = (ZG - 1 - my_row // stride % ZG) * x.shape[0]
        return lax.dynamic_slice_in_dim(jnp.concatenate(ring + ring), first, ZG * x.shape[0], 0)

    def exchange_flat(x):
        return lax.all_to_all(x, "rays", 0, 0, tiled=True, axis_index_groups=flat_groups)

    column = jnp.stack([tile_density] + [along_z(tile_density, d) for d in range(1, ZG)])

    own_map = lax.dynamic_index_in_dim(long_maps[0], plane, 0, keepdims=False)
    own_map = own_map.transpose(1, 2, 0).reshape(level, 2 * extent // level, extent)
    owner = lax.dynamic_index_in_dim(map_owner, plane, 0, keepdims=False)
    pieces = exchange_flat(own_map)
    piece = lax.dynamic_index_in_dim(pieces, owner % level, 0, keepdims=False)

    level_lists = lax.dynamic_slice(tile_lists, (my_z * level, 0, 0), (level, planes, list_len))
    owners = level_lists // tile_dev
    key = jnp.arange(list_len, dtype=jnp.int32) * tile_dev + level_lists % tile_dev
    column_owner = (my_z - jnp.arange(ZG, dtype=jnp.int32)) % ZG * level + my_xy
    mine = owners[:, :, None, :] == column_owner[None, None, :, None]
    first = jnp.min(jnp.where(mine, key[:, :, None, :], tile_dev * list_len), axis=3) % tile_dev
    last = jnp.max(jnp.where(mine, key[:, :, None, :], 0), axis=3) % tile_dev
    wanted = jnp.stack([first, last], axis=3)[..., None, None]
    by_plane = column.transpose(1, 0, 2, 3, 4)
    outgoing = jnp.broadcast_to(
        by_plane[None, :, :, None, 0], (level, planes, ZG, 2, strip, side)
    )
    for t in range(1, tile_dev):
        outgoing = jnp.where(wanted == t, by_plane[None, :, :, None, t], outgoing)
    small = jnp.concatenate(
        [block_slots[:, None, :], block_windows // SUB, block_windows % SUB], axis=1
    ).reshape(planes, 1, 5 * blocks)
    small = jnp.pad(small, ((0, 0), (0, 3), (0, 128 - 5 * blocks)))
    cells = jnp.concatenate([fine_cells, long_cells], axis=1)
    ray_info = jnp.concatenate([cells, small], axis=2).astype(BF)
    arrived = [lax.dynamic_index_in_dim(ray_info, plane, 0, keepdims=False)]
    for d in range(1, planes):
        pairs = [(i, (i + d) % planes) for i in range(planes)]
        sent = lax.dynamic_index_in_dim(ray_info, (plane + d) % planes, 0, keepdims=False)
        arrived.append(lax.ppermute(sent, "planes", pairs))
    arrived = jnp.stack(arrived)
    outgoing, piece, arrived = lax.optimization_barrier((outgoing, piece, arrived))
    cells = arrived[:, :, :rays_here].astype(F32)
    small = arrived[:, 0, rays_here : rays_here + 5 * blocks].astype(jnp.int32)
    small = small.reshape(planes, 5, blocks)
    turn = (plane - jnp.arange(planes)) % planes
    small = jnp.sum(
        jnp.where(turn[:, None] == jnp.arange(planes), 1, 0)[:, :, None, None] * small[None], axis=1
    )
    slots = small[:, 0].reshape(planes * blocks)
    starts = (small[:, 1:3] * SUB + small[:, 3:5]).transpose(1, 0, 2).reshape(2, planes * blocks)
    whose = plane.reshape(1)

    incoming = lax.all_to_all(
        outgoing.reshape(level * planes, ZG * 2, strip, side),
        ("rays", "planes"),
        0,
        0,
        tiled=True,
        axis_index_groups=[
            list(range(z * level * planes, (z + 1) * level * planes)) for z in range(ZG)
        ],
    ).reshape(level, planes, ZG * 2, strip, side)

    distance = (my_z - owner // level) % ZG
    chosen = piece
    for d in range(1, ZG):
        chosen = jnp.where(distance == d, along_z(piece, d), chosen)

    my_list = lax.dynamic_slice(tile_lists, (my_row, plane, 0), (1, 1, list_len))[0, 0]
    my_owner = my_list // tile_dev
    place = jnp.arange(list_len, dtype=jnp.int32)
    repeat = (my_owner[:, None] == my_owner[None, :]) & (place[:, None] > place[None, :])
    rank = jnp.max(repeat.astype(jnp.int32), axis=1)
    entry = my_owner % level * (2 * ZG) + (my_z - my_owner // level) % ZG * 2 + rank

    whole = gathered(gathered(chosen, 1), ZG).reshape(2, extent, extent)

    select = (jnp.arange(8 * SUB)[None, :] // SUB == jnp.arange(SUB)[:, None]).astype(BF)
    smooth_table, slope_table = kernel_tables(side)
    left = jnp.concatenate([smooth_table, slope_table], axis=0)
    halves = 2
    wide = rays_here // halves
    vmem = pl.BlockSpec(memory_space=pltpu.VMEM)
    anywhere = pl.BlockSpec(memory_space=pl.ANY)
    params = pltpu.CompilerParams(vmem_limit_bytes=48 << 20)

    def cell_spec(h=None):
        def index(g, whose, *_):
            src = g if h is not None else g // halves
            return (whose[0] + planes - src) % planes, 0, h if h is not None else g % halves

        return pl.BlockSpec((1, 4, wide), index)

    long_corners = pl.pallas_call(
        long_kernel,
        out_shape=jax.ShapeDtypeStruct((planes, 8, rays_here), BF),
        grid_spec=pltpu.PrefetchScalarGridSpec(
            num_scalar_prefetch=2,
            grid=(planes * halves,),
            in_specs=[vmem, cell_spec(), vmem],
            out_specs=pl.BlockSpec((1, 8, wide), lambda g, *_: (g // halves, 0, g % halves)),
        ),
        compiler_params=params,
        name="long_gather",
    )(whose, starts, whole, cells, select)
    incoming, long_corners = lax.optimization_barrier((incoming, long_corners))
    received = lax.all_to_all(long_corners, "planes", 0, 0, tiled=True)
    long_corners = received
    outputs = (
        jax.ShapeDtypeStruct((planes, 2, rays_here), F32),
        jax.ShapeDtypeStruct((2, rays_here), F32),
    )
    results = ()
    part = 2048
    for h in range(halves):
        fine_corners = pl.pallas_call(
            functools.partial(fine_kernel, h, halves),
            out_shape=jax.ShapeDtypeStruct((planes, 8, wide), BF),
            grid_spec=pltpu.PrefetchScalarGridSpec(
                num_scalar_prefetch=3,
                grid=(planes,),
                in_specs=[vmem, cell_spec(h), vmem, vmem, vmem, vmem],
                out_specs=pl.BlockSpec((1, 8, wide), lambda g, *_: (g, 0, 0)),
            ),
            compiler_params=params,
            name=f"fine_gather_{h}",
        )(whose, slots, entry, incoming, cells, left, with_next(slope_table), with_next(smooth_table), select)
        fine_corners, incoming, received = lax.optimization_barrier((fine_corners, incoming, received))
        received = lax.all_to_all(fine_corners, "planes", 0, 0, tiled=True)
        steps = wide // part
        results = pl.pallas_call(
            functools.partial(final_kernel, len(results)),
            out_shape=outputs,
            grid=(steps,),
            in_specs=[
                pl.BlockSpec((planes, 8, part), lambda g: (0, 0, g)),
                pl.BlockSpec((planes, 8, part), lambda g, h=h: (0, 0, h * steps + g)),
                pl.BlockSpec((planes, 4, part), lambda g, h=h: (0, 0, h * steps + g)),
                *[anywhere for _ in results],
            ],
            out_specs=(
                pl.BlockSpec((planes, 2, part), lambda g, h=h: (0, 0, h * steps + g)),
                pl.BlockSpec((2, part), lambda g, h=h: (0, h * steps + g)),
            ),
            input_output_aliases={3 + i: i for i in range(len(results))},
            name=f"lens_sum_{h}",
        )(received, long_corners, fractions, *results)
    return tuple(results)


def solution(mesh):
    return jax.shard_map(
        per_device,
        mesh=mesh,
        in_specs=(
            P(None, "rays", "planes", None),
            P("rays", None, None, None, None),
            P(),
            P(),
            P(None, ("rays", "planes")),
            P(None, None, ("rays", "planes")),
            P(None, None, ("rays", "planes")),
            P(None, None, ("rays", "planes")),
            P(None, None, ("rays", "planes")),
        ),
        out_specs=(P(None, None, ("rays", "planes")), P(None, ("rays", "planes"))),
        check_vma=False,
    )
```

```python
import functools

import jax
import jax.numpy as jnp
from jax import lax
from jax.experimental import pallas as pl
from jax.experimental.pallas import tpu as pltpu
from jax.sharding import PartitionSpec as P

RATIO = 16
BF = jnp.bfloat16
F32 = jnp.float32
SUB = 16
ZG = 4
TAPS = 6


def kernel_tables(side):
    indices = jnp.arange(side, dtype=jnp.int32)
    offset = (indices[:, None] - indices[None, :]).astype(F32)
    tap_offsets = jnp.arange(-TAPS, TAPS + 1, dtype=jnp.int32).astype(F32)
    tap_total = jnp.sum(jnp.exp(-tap_offsets * tap_offsets / 8.0))
    inside = jnp.abs(offset) <= TAPS
    weight = jnp.where(inside, jnp.exp(-offset * offset / 8.0), 0.0) / tap_total
    smooth_table = weight.astype(BF)
    slope_table = (6.0 * offset * weight / 4.0).astype(BF)
    return (smooth_table, slope_table)


def with_next(table):
    following = jnp.concatenate([table[1:], jnp.zeros_like(table[:1])], axis=0)
    return jnp.concatenate([table.T, following.T], axis=1)


def onehot_tiles(row, tiles, width):
    wide = jnp.broadcast_to(row, (SUB, width)).astype(BF)
    place = lax.broadcasted_iota(jnp.int32, (SUB, width), 0).astype(F32)
    one = jnp.ones((SUB, width), BF)
    zero = jnp.zeros((SUB, width), BF)
    return [
        jnp.where(wide == (place + float(SUB * t)).astype(BF), one, zero) for t in range(tiles)
    ]


def corner_sums(found, columns, select):
    rows = found.shape[0] // 4
    half = found.shape[1] // 2
    results = []
    for h in range(2):
        lanes = slice(h * half, (h + 1) * half)
        column = columns[:, lanes]
        tile_of = [jnp.floor((column + step) * (1.0 / SUB)) for step in (0.0, 1.0)]
        wide = [jnp.broadcast_to(t, (SUB, half)).astype(BF) for t in tile_of]
        kept = [[None, None] for _ in range(4)]
        for t in range(rows // SUB):
            hit = [w == float(t) for w in wide]
            for i in range(4):
                low = found[i * rows + t * SUB : i * rows + (t + 1) * SUB, lanes].astype(BF)
                for s in range(2):
                    kept[i][s] = low if t == 0 else jnp.where(hit[s], low, kept[i][s])
        hot = [onehot_tiles(column + s - SUB * tile_of[s], 1, half)[0] for s in range(2)]
        stacked = jnp.concatenate([kept[i][s] * hot[s] for i in range(4) for s in range(2)], axis=0)
        results.append(jnp.dot(select, stacked, preferred_element_type=F32)[:8])
    return jnp.concatenate(results, axis=1)


def pipelined(count, stages):
    held = {}
    for turn in range(count + len(stages) - 1):
        for s, stage in enumerate(stages):
            item = turn - s
            if 0 <= item < count:
                held[item] = stage(item, held.get(item))


def fine_kernel(whose_ref, slot_ref, entry_ref, tiles_ref, cells_ref, left_ref, slope_ref, smooth_ref, select_ref, out_ref):
    step = pl.program_id(0)
    width = 512
    per_step = out_ref.shape[2] // width
    places, strips = tiles_ref.shape[1:3]
    side = tiles_ref.shape[4]

    def lanes(b):
        return slice(b * width, (b + 1) * width)

    def columns_done(b, _):
        entry = entry_ref[slot_ref[step * per_step + b]]
        source, place = entry // strips, entry % strips
        density = jnp.concatenate([tiles_ref[source, i, place] for i in range(places)], axis=0)
        return lax.dot_general(
            left_ref[...], density, (((1,), (1,)), ((), ())), preferred_element_type=F32
        ).astype(BF)

    def fields(b, partial):
        along_x = jnp.dot(partial[:side], slope_ref[...], preferred_element_type=F32).astype(BF)
        along_y = jnp.dot(partial[side:], smooth_ref[...], preferred_element_type=F32).astype(BF)
        return jnp.concatenate(
            [along_x[:, :side], along_y[:, :side], along_x[:, side:], along_y[:, side:]], axis=0
        )

    def gather_rows(b, table):
        hot = jnp.concatenate(onehot_tiles(cells_ref[0, 0:1, lanes(b)], side // SUB, width), axis=0)
        return jnp.dot(table, hot, preferred_element_type=F32)

    def gather_columns(b, found):
        corners = corner_sums(found, cells_ref[0, 1:2, lanes(b)], select_ref[...])
        out_ref[0, :, lanes(b)] = corners.astype(BF)

    pipelined(per_step, (columns_done, fields, gather_rows, gather_columns))


def long_kernel(part, parts, whose_ref, start_ref, map_ref, cells_ref, select_ref, out_ref):
    step = pl.program_id(0)
    width = 512
    per_step = out_ref.shape[2] // width
    extent = map_ref.shape[1]
    side = 128
    rows = side + SUB

    def lanes(b):
        return slice(b * width, (b + 1) * width)

    def bases(b):
        block = (step * parts + part) * per_step + b
        row_start = start_ref[0, block]
        col_start = start_ref[1, block]
        row_base = jnp.minimum(row_start // side, extent // side - 2) * side
        col_base = jnp.minimum(col_start // SUB, (extent - rows) // SUB) * SUB
        return row_start, pl.multiple_of(row_base, side), col_start, pl.multiple_of(col_base, SUB)

    def gather_rows(b, _):
        row_start, row_base, _, col_base = bases(b)
        take = (pl.ds(col_base, rows), pl.ds(row_base, 2 * side))
        table = jnp.concatenate([map_ref[(0, *take)], map_ref[(1, *take)]], axis=0)
        table = jnp.concatenate([table, pltpu.roll(table, 2 * side - 1, axis=1)], axis=0)
        row = cells_ref[0, 2:3, lanes(b)] + (row_start - row_base).astype(F32)
        hot = jnp.concatenate(onehot_tiles(row, 2 * side // SUB, width), axis=0)
        return jnp.dot(table, hot, preferred_element_type=F32)

    def gather_columns(b, found):
        _, _, col_start, col_base = bases(b)
        col = cells_ref[0, 3:4, lanes(b)] + (col_start - col_base).astype(F32)
        out_ref[0, :, lanes(b)] = corner_sums(found, col, select_ref[...]).astype(BF)

    pipelined(per_step, (gather_rows, gather_columns))


def pick_kernel(wanted_ref, *refs):
    sources, out_ref = refs[:-1], refs[-1]
    step = pl.program_id(0)
    count, planes, places = out_ref.shape[:3]
    each = places // len(sources)
    for i in range(count):
        for k in range(planes):
            for j in range(places):
                tile = wanted_ref[step * count + i, k * places + j]
                out_ref[i, k, j] = sources[j // each][k, tile]


def table_value(corners, p, q):
    rw0 = (1.0 - p).astype(BF).astype(F32)
    rw1 = p.astype(BF).astype(F32)
    cw0, cw1 = 1.0 - q, q
    v = [corners[i : i + 1] for i in range(8)]
    along_x = (rw0 * v[0] + rw1 * v[4]) * cw0 + (rw0 * v[1] + rw1 * v[5]) * cw1
    along_y = (rw0 * v[2] + rw1 * v[6]) * cw0 + (rw0 * v[3] + rw1 * v[7]) * cw1
    return along_x, along_y


def lens_shift(previous, target):
    shift_x, shift_y = 0.0, 0.0
    for earlier, (x, y) in enumerate(previous):
        factor = (target - earlier) / target
        shift_x, shift_y = shift_x - factor * x, shift_y - factor * y
    return shift_x, shift_y


def final_kernel(held, fine_ref, long_ref, frac_ref, *refs):
    deflection_ref, source_ref = refs[held:]
    planes = fine_ref.shape[0]
    found = []
    for k in range(planes):
        frac = frac_ref[k]
        sx, sy = lens_shift(found, k)
        fx, fy = table_value(fine_ref[k].astype(F32), frac[0:1] + sx, frac[1:2] + sy)
        lx, ly = table_value(
            long_ref[k].astype(F32), frac[2:3] + sx / RATIO, frac[3:4] + sy / RATIO
        )
        found.append((fx + lx, fy + ly))
        deflection_ref[k, 0:1] = found[k][0]
        deflection_ref[k, 1:2] = found[k][1]
    sx, sy = lens_shift(found, planes)
    source_ref[0:1] = sx
    source_ref[1:2] = sy


def per_device(
    tile_density,
    long_maps,
    map_owner,
    tile_lists,
    block_slots,
    block_windows,
    fine_cells,
    long_cells,
    fractions,
):
    my_row = lax.axis_index("rays")
    plane = lax.axis_index("planes")
    planes, tile_dev, strip, side = tile_density.shape
    extent = long_maps.shape[2]
    list_len = tile_lists.shape[2]
    rays_here = fine_cells.shape[2]
    blocks = block_slots.shape[1]
    ray_count = lax.axis_size("rays")
    level = ray_count // ZG
    my_z, my_xy = my_row // level, my_row % level
    flat_groups = [[z * level + i for i in range(level)] for z in range(ZG)]

    def moved(x, stride, d):
        pairs = [(r, r + ((r // stride + d) % ZG - r // stride % ZG) * stride) for r in range(ray_count)]
        return lax.ppermute(x, "rays", pairs)

    def along_z(x, d):
        return moved(x, level, d)

    def exchange_flat(x):
        return lax.all_to_all(x, "rays", 0, 0, tiled=True, axis_index_groups=flat_groups)

    column = [tile_density] + [along_z(tile_density, d) for d in range(1, ZG)]

    own_map = lax.dynamic_index_in_dim(long_maps[0], plane, 0, keepdims=False)
    own_map = own_map.transpose(1, 2, 0).reshape(level, 2 * extent // level, extent)
    owner = lax.dynamic_index_in_dim(map_owner, plane, 0, keepdims=False)
    pieces = exchange_flat(own_map)
    piece = lax.dynamic_index_in_dim(pieces, owner % level, 0, keepdims=False)

    level_lists = lax.dynamic_slice(tile_lists, (my_z * level, 0, 0), (level, planes, list_len))
    owners = level_lists // tile_dev
    key = jnp.arange(list_len, dtype=jnp.int32) * tile_dev + level_lists % tile_dev
    column_owner = (my_z - jnp.arange(ZG, dtype=jnp.int32)) % ZG * level + my_xy
    mine = owners[:, :, None, :] == column_owner[None, None, :, None]
    first = jnp.min(jnp.where(mine, key[:, :, None, :], tile_dev * list_len), axis=3) % tile_dev
    last = jnp.max(jnp.where(mine, key[:, :, None, :], 0), axis=3) % tile_dev
    wanted = jnp.stack([first, last], axis=3).reshape(level, planes * ZG * 2)
    outgoing = pl.pallas_call(
        pick_kernel,
        out_shape=jax.ShapeDtypeStruct((level, planes, ZG * 2, strip, side), BF),
        grid_spec=pltpu.PrefetchScalarGridSpec(
            num_scalar_prefetch=1,
            grid=(level // 2,),
            in_specs=[pl.BlockSpec(memory_space=pltpu.VMEM) for _ in column],
            out_specs=pl.BlockSpec((2, planes, ZG * 2, strip, side), lambda g, *_: (g, 0, 0, 0, 0)),
        ),
        name="pick_strips",
    )(wanted, *column)

    small = jnp.concatenate(
        [block_slots[:, None, :], block_windows // SUB, block_windows % SUB], axis=1
    ).reshape(planes, 1, 5 * blocks)
    small = jnp.pad(small, ((0, 0), (0, 3), (0, 128 - 5 * blocks)))
    cells = jnp.concatenate([fine_cells, long_cells], axis=1)
    ray_info = jnp.concatenate([cells, small], axis=2).astype(BF)
    arrived = [lax.dynamic_index_in_dim(ray_info, plane, 0, keepdims=False)]
    for d in range(1, planes):
        pairs = [(i, (i + d) % planes) for i in range(planes)]
        sent = lax.dynamic_index_in_dim(ray_info, (plane + d) % planes, 0, keepdims=False)
        arrived.append(lax.ppermute(sent, "planes", pairs))
    arrived = jnp.stack(arrived)
    outgoing, piece, arrived = lax.optimization_barrier((outgoing, piece, arrived))
    cells = arrived[:, :, :rays_here].astype(F32)
    small = arrived[:, 0, rays_here : rays_here + 5 * blocks].astype(jnp.int32)
    small = small.reshape(planes, 5, blocks)
    turn = (plane - jnp.arange(planes)) % planes
    small = jnp.sum(
        jnp.where(turn[:, None] == jnp.arange(planes), 1, 0)[:, :, None, None] * small[None], axis=1
    )
    slots = small[:, 0].reshape(planes * blocks)
    starts = (small[:, 1:3] * SUB + small[:, 3:5]).transpose(1, 0, 2).reshape(2, planes * blocks)
    whose = plane.reshape(1)

    incoming = lax.all_to_all(
        outgoing.reshape(level * planes, ZG * 2, strip, side),
        ("rays", "planes"),
        0,
        0,
        tiled=True,
        axis_index_groups=[
            list(range(z * level * planes, (z + 1) * level * planes)) for z in range(ZG)
        ],
    ).reshape(level, planes, ZG * 2, strip, side)

    distance = (my_z - owner // level) % ZG
    chosen = piece
    for d in range(1, ZG):
        chosen = jnp.where(distance == d, along_z(piece, d), chosen)

    my_list = lax.dynamic_slice(tile_lists, (my_row, plane, 0), (1, 1, list_len))[0, 0]
    my_owner = my_list // tile_dev
    place = jnp.arange(list_len, dtype=jnp.int32)
    repeat = (my_owner[:, None] == my_owner[None, :]) & (place[:, None] > place[None, :])
    rank = jnp.max(repeat.astype(jnp.int32), axis=1)
    entry = my_owner % level * (2 * ZG) + (my_z - my_owner // level) % ZG * 2 + rank

    chosen, incoming = lax.optimization_barrier((chosen, incoming))
    whole = exchange_flat(jnp.broadcast_to(chosen[None], (level, *chosen.shape)))
    whole = whole.reshape(2, extent, extent)

    select = (jnp.arange(8 * SUB)[None, :] // SUB == jnp.arange(SUB)[:, None]).astype(BF)
    smooth_table, slope_table = kernel_tables(side)
    left = jnp.concatenate([smooth_table, slope_table], axis=0)
    halves = 2
    wide = rays_here // halves
    vmem = pl.BlockSpec(memory_space=pltpu.VMEM)
    anywhere = pl.BlockSpec(memory_space=pl.ANY)
    params = pltpu.CompilerParams(vmem_limit_bytes=48 << 20)

    def cell_spec(h=None):
        def index(g, whose, *_):
            src = g if h is not None else g // halves
            return (whose[0] + planes - src) % planes, 0, h if h is not None else g % halves

        return pl.BlockSpec((1, 4, wide), index)

    fine_corners = pl.pallas_call(
        fine_kernel,
        out_shape=jax.ShapeDtypeStruct((planes, 8, rays_here), BF),
        grid_spec=pltpu.PrefetchScalarGridSpec(
            num_scalar_prefetch=3,
            grid=(planes * halves,),
            in_specs=[vmem, cell_spec(), vmem, vmem, vmem, vmem],
            out_specs=pl.BlockSpec((1, 8, wide), lambda g, *_: (g // halves, 0, g % halves)),
        ),
        compiler_params=params,
        name="fine_gather",
    )(whose, slots, entry, incoming, cells, left, with_next(slope_table), with_next(smooth_table), select)
    fine_corners, whole = lax.optimization_barrier((fine_corners, whole))
    fine_corners = lax.all_to_all(fine_corners, "planes", 0, 0, tiled=True)
    received = fine_corners
    outputs = (
        jax.ShapeDtypeStruct((planes, 2, rays_here), F32),
        jax.ShapeDtypeStruct((2, rays_here), F32),
    )
    results = ()
    part = 2048
    for h in range(halves):
        long_corners = pl.pallas_call(
            functools.partial(long_kernel, h, halves),
            out_shape=jax.ShapeDtypeStruct((planes, 8, wide), BF),
            grid_spec=pltpu.PrefetchScalarGridSpec(
                num_scalar_prefetch=2,
                grid=(planes,),
                in_specs=[vmem, cell_spec(h), vmem],
                out_specs=pl.BlockSpec((1, 8, wide), lambda g, *_: (g, 0, 0)),
            ),
            compiler_params=params,
            name=f"long_gather_{h}",
        )(whose, starts, whole, cells, select)
        long_corners, whole, received = lax.optimization_barrier((long_corners, whole, received))
        received = lax.all_to_all(long_corners, "planes", 0, 0, tiled=True)
        steps = wide // part
        results = pl.pallas_call(
            functools.partial(final_kernel, len(results)),
            out_shape=outputs,
            grid=(steps,),
            in_specs=[
                pl.BlockSpec((planes, 8, part), lambda g, h=h: (0, 0, h * steps + g)),
                pl.BlockSpec((planes, 8, part), lambda g: (0, 0, g)),
                pl.BlockSpec((planes, 4, part), lambda g, h=h: (0, 0, h * steps + g)),
                *[anywhere for _ in results],
            ],
            out_specs=(
                pl.BlockSpec((planes, 2, part), lambda g, h=h: (0, 0, h * steps + g)),
                pl.BlockSpec((2, part), lambda g, h=h: (0, h * steps + g)),
            ),
            input_output_aliases={3 + i: i for i in range(len(results))},
            name=f"lens_sum_{h}",
        )(fine_corners, received, fractions, *results)
    return tuple(results)


def solution(mesh):
    return jax.shard_map(
        per_device,
        mesh=mesh,
        in_specs=(
            P(None, "rays", "planes", None),
            P("rays", None, None, None, None),
            P(),
            P(),
            P(None, ("rays", "planes")),
            P(None, None, ("rays", "planes")),
            P(None, None, ("rays", "planes")),
            P(None, None, ("rays", "planes")),
            P(None, None, ("rays", "planes")),
        ),
        out_specs=(P(None, None, ("rays", "planes")), P(None, ("rays", "planes"))),
        check_vma=False,
    )
```

```python
import functools

import jax
import jax.numpy as jnp
from jax import lax
from jax.experimental import pallas as pl
from jax.experimental.pallas import tpu as pltpu
from jax.sharding import PartitionSpec as P

RATIO = 16
BF = jnp.bfloat16
F32 = jnp.float32
SUB = 16
ZG = 4
TAPS = 6
HALF = 64


def kernel_tables(side):
    indices = jnp.arange(side, dtype=jnp.int32)
    offset = (indices[:, None] - indices[None, :]).astype(F32)
    tap_offsets = jnp.arange(-TAPS, TAPS + 1, dtype=jnp.int32).astype(F32)
    tap_total = jnp.sum(jnp.exp(-tap_offsets * tap_offsets / 8.0))
    inside = jnp.abs(offset) <= TAPS
    weight = jnp.where(inside, jnp.exp(-offset * offset / 8.0), 0.0) / tap_total
    smooth_table = weight.astype(BF)
    slope_table = (6.0 * offset * weight / 4.0).astype(BF)
    return (smooth_table, slope_table)


def with_next(table):
    following = jnp.concatenate([table[1:], jnp.zeros_like(table[:1])], axis=0)
    return jnp.concatenate([table.T, following.T], axis=1)


def onehot_tiles(row, tiles, width):
    wide = jnp.broadcast_to(row, (SUB, width)).astype(BF)
    place = lax.broadcasted_iota(jnp.int32, (SUB, width), 0).astype(F32)
    one = jnp.ones((SUB, width), BF)
    zero = jnp.zeros((SUB, width), BF)
    return [
        jnp.where(wide == (place + float(SUB * t)).astype(BF), one, zero) for t in range(tiles)
    ]


def two_halves(parts):
    return jnp.concatenate(
        [jnp.concatenate([p[: HALF + SUB], p[HALF:]], axis=1) for p in parts], axis=0
    )


def split_columns(row, column):
    upper = jnp.where(column >= float(HALF), 1.0, 0.0)
    return row + 2 * HALF * upper, column - HALF * upper


def corner_values(found, columns):
    rows, width = found.shape[0] // 4, found.shape[1]
    lane = 128
    half = 2 * lane
    results = []
    for h in range(width // half):
        lanes = slice(h * half, (h + 1) * half)
        column = columns[:, lanes]
        tile_of = [jnp.floor((column + step) * (1.0 / SUB)) for step in (0.0, 1.0)]
        wide = [jnp.broadcast_to(t, (SUB, half)).astype(BF) for t in tile_of]
        kept = [[None, None] for _ in range(4)]
        for t in range(rows // SUB):
            hit = [w == float(t) for w in wide]
            for i in range(4):
                low = found[i * rows + t * SUB : i * rows + (t + 1) * SUB, lanes].astype(BF)
                for s in range(2):
                    kept[i][s] = low if t == 0 else jnp.where(hit[s], low, kept[i][s])
        inner = [
            jnp.broadcast_to(column + s - SUB * tile_of[s], (8, half)).astype(jnp.int32)
            for s in range(2)
        ]
        for w in range(half // lane):
            cut = slice(w * lane, (w + 1) * lane)
            sub = lax.broadcasted_iota(jnp.int32, (8, lane), 0)
            value = None
            for s in range(2):
                row = inner[s][:, cut]
                upper, row = row >= 8, row & 7
                for i in range(4):
                    both = kept[i][s][:, cut].astype(F32)
                    one = jnp.where(upper, both[8:], both[:8])
                    one = jnp.take_along_axis(one, row, axis=0, mode="promise_in_bounds")
                    value = one if value is None else jnp.where(sub == 2 * i + s, one, value)
            results.append(value)
    return jnp.concatenate(results, axis=1)


def pipelined(count, stages):
    held = {}
    for turn in range(count + len(stages) - 1):
        for s, stage in enumerate(stages):
            item = turn - s
            if 0 <= item < count:
                held[item] = stage(item, held.get(item))


def fine_kernel(whose_ref, slot_ref, entry_ref, tiles_ref, cells_ref, left_ref, slope_ref, smooth_ref, out_ref):
    step = pl.program_id(0)
    width = 512
    per_step = out_ref.shape[2] // width
    places, strips = tiles_ref.shape[1:3]
    side = tiles_ref.shape[4]

    def lanes(b):
        return slice(b * width, (b + 1) * width)

    def columns_done(b):
        pair = []
        for i in (b, b + 1):
            entry = entry_ref[slot_ref[step * per_step + i]]
            source, place = entry // strips, entry % strips
            pair += [tiles_ref[source, k, place] for k in range(places)]
        return lax.dot_general(
            left_ref[...],
            jnp.concatenate(pair, axis=0),
            (((1,), (1,)), ((), ())),
            preferred_element_type=F32,
        ).astype(BF)

    def fields(partial):
        partial = [partial[:, :side], partial[:, side:]]
        along_x = jnp.concatenate([p[:side] for p in partial], axis=0)
        along_y = jnp.concatenate([p[side:] for p in partial], axis=0)
        along_x = jnp.dot(along_x, slope_ref[...], preferred_element_type=F32).astype(BF)
        along_y = jnp.dot(along_y, smooth_ref[...], preferred_element_type=F32).astype(BF)
        past = jnp.zeros((SUB, side), BF)
        tables = []
        for i in range(2):
            x, y = (a[i * side : (i + 1) * side] for a in (along_x, along_y))
            four = (x[:, :side], y[:, :side], x[:, side:], y[:, side:])
            tables.append(two_halves([jnp.concatenate([f, past], axis=0) for f in four]))
        return tables

    def gather_rows(b, table):
        row, _ = split_columns(cells_ref[0, 0:1, lanes(b)], cells_ref[0, 1:2, lanes(b)])
        hot = jnp.concatenate(onehot_tiles(row, 2 * side // SUB, width), axis=0)
        return jnp.dot(table, hot, preferred_element_type=F32)

    def gather_columns(b, found):
        _, column = split_columns(cells_ref[0, 0:1, lanes(b)], cells_ref[0, 1:2, lanes(b)])
        out_ref[0, :, lanes(b)] = corner_values(found, column).astype(BF)

    partial, tables, found = {}, {}, {}
    for turn in range(per_step + 4):
        if turn < per_step and turn % 2 == 0:
            partial[turn] = columns_done(turn)
        b = turn - 2
        if 0 <= b < per_step and b % 2 == 0:
            tables[b], tables[b + 1] = fields(partial.pop(b))
        b = turn - 3
        if 0 <= b < per_step:
            found[b] = gather_rows(b, tables.pop(b))
        b = turn - 4
        if 0 <= b < per_step:
            gather_columns(b, found.pop(b))


def long_kernel(part, parts, whose_ref, start_ref, map_ref, cells_ref, out_ref):
    step = pl.program_id(0)
    width = 512
    per_step = out_ref.shape[2] // width
    extent = map_ref.shape[1]
    side = 128
    rows = side + SUB

    def lanes(b):
        return slice(b * width, (b + 1) * width)

    def bases(b):
        block = (step * parts + part) * per_step + b
        row_start = start_ref[0, block]
        col_start = start_ref[1, block]
        row_base = jnp.minimum(row_start // side, extent // side - 2) * side
        col_base = jnp.minimum(col_start // SUB, (extent - rows) // SUB) * SUB
        return row_start, pl.multiple_of(row_base, side), col_start, pl.multiple_of(col_base, SUB)

    def place(b):
        _, _, col_start, col_base = bases(b)
        column = cells_ref[0, 3:4, lanes(b)] + (col_start - col_base).astype(F32)
        return split_columns(cells_ref[0, 2:3, lanes(b)], column)

    def gather_rows(b, _):
        row_start, row_base, _, col_base = bases(b)
        offset = row_start - row_base
        parts = []
        for turn in ((2 * side - offset) & (2 * side - 1), 2 * side - 1 - offset):
            for i in range(2):
                window = map_ref[i, pl.ds(col_base, rows), pl.ds(row_base, 2 * side)]
                parts.append(pltpu.roll(window, turn, axis=1)[:, :side])
        row, _ = place(b)
        hot = jnp.concatenate(onehot_tiles(row, 2 * side // SUB, width), axis=0)
        return jnp.dot(two_halves(parts), hot, preferred_element_type=F32)

    def gather_columns(b, found):
        _, column = place(b)
        out_ref[0, :, lanes(b)] = corner_values(found, column).astype(BF)

    pipelined(per_step, (gather_rows, gather_columns))


def pick_kernel(wanted_ref, *refs):
    sources, out_ref = refs[:-1], refs[-1]
    step = pl.program_id(0)
    count, planes, places = out_ref.shape[:3]
    each = places // len(sources)
    for i in range(count):
        for k in range(planes):
            for j in range(places):
                tile = wanted_ref[step * count + i, k * places + j]
                out_ref[i, k, j] = sources[j // each][k, tile]


def weighted(corners, p, q):
    sub = lax.broadcasted_iota(jnp.int32, corners.shape, 0)
    p, q = jnp.broadcast_to(p, corners.shape), jnp.broadcast_to(q, corners.shape)
    row = jnp.where(sub < 4, 1.0 - p, p).astype(BF).astype(F32)
    column = jnp.where(sub % 2 == 0, 1.0 - q, q)
    return corners * row * column


def lens_shift(previous, target):
    shift = 0.0
    for earlier, deflection in enumerate(previous):
        shift = shift - (target - earlier) / target * deflection
    return shift


def final_kernel(held, fine_ref, long_ref, frac_ref, *refs):
    deflection_ref, source_ref = refs[held:]
    planes = fine_ref.shape[0]
    found = []
    for k in range(planes):
        at = frac_ref[k]
        p, q, p2, q2 = (at[i : i + 1] for i in range(4))
        if k > 0:
            shift = lens_shift(found, k)
            sx, sy = shift[0:1], shift[2:3]
            p, q, p2, q2 = p + sx, q + sy, p2 + sx / RATIO, q2 + sy / RATIO
        terms = weighted(fine_ref[k].astype(F32), p, q) + weighted(long_ref[k].astype(F32), p2, q2)
        terms = terms + pltpu.roll(terms, 4, axis=0)
        terms = terms + pltpu.roll(terms, 7, axis=0)
        found.append(terms)
        deflection_ref[k, 0:1] = terms[0:1]
        deflection_ref[k, 1:2] = terms[2:3]
    shift = lens_shift(found, planes)
    source_ref[0:1] = shift[0:1]
    source_ref[1:2] = shift[2:3]


def per_device(
    tile_density,
    long_maps,
    map_owner,
    tile_lists,
    block_slots,
    block_windows,
    fine_cells,
    long_cells,
    fractions,
):
    my_row = lax.axis_index("rays")
    plane = lax.axis_index("planes")
    planes, tile_dev, strip, side = tile_density.shape
    extent = long_maps.shape[2]
    list_len = tile_lists.shape[2]
    rays_here = fine_cells.shape[2]
    blocks = block_slots.shape[1]
    ray_count = lax.axis_size("rays")
    level = ray_count // ZG
    my_z, my_xy = my_row // level, my_row % level
    flat_groups = [[z * level + i for i in range(level)] for z in range(ZG)]

    def moved(x, stride, d):
        pairs = [(r, r + ((r // stride + d) % ZG - r // stride % ZG) * stride) for r in range(ray_count)]
        return lax.ppermute(x, "rays", pairs)

    def along_z(x, d):
        return moved(x, level, d)

    def exchange_flat(x):
        return lax.all_to_all(x, "rays", 0, 0, tiled=True, axis_index_groups=flat_groups)

    column = [tile_density] + [along_z(tile_density, d) for d in range(1, ZG)]

    own_map = lax.dynamic_index_in_dim(long_maps[0], plane, 0, keepdims=False)
    own_map = own_map.transpose(1, 2, 0).reshape(level, 2 * extent // level, extent)
    owner = lax.dynamic_index_in_dim(map_owner, plane, 0, keepdims=False)
    pieces = exchange_flat(own_map)
    piece = lax.dynamic_index_in_dim(pieces, owner % level, 0, keepdims=False)

    level_lists = lax.dynamic_slice(tile_lists, (my_z * level, 0, 0), (level, planes, list_len))
    owners = level_lists // tile_dev
    key = jnp.arange(list_len, dtype=jnp.int32) * tile_dev + level_lists % tile_dev
    column_owner = (my_z - jnp.arange(ZG, dtype=jnp.int32)) % ZG * level + my_xy
    mine = owners[:, :, None, :] == column_owner[None, None, :, None]
    first = jnp.min(jnp.where(mine, key[:, :, None, :], tile_dev * list_len), axis=3) % tile_dev
    last = jnp.max(jnp.where(mine, key[:, :, None, :], 0), axis=3) % tile_dev
    wanted = jnp.stack([first, last], axis=3).reshape(level, planes * ZG * 2)
    outgoing = pl.pallas_call(
        pick_kernel,
        out_shape=jax.ShapeDtypeStruct((level, planes, ZG * 2, strip, side), BF),
        grid_spec=pltpu.PrefetchScalarGridSpec(
            num_scalar_prefetch=1,
            grid=(level // 2,),
            in_specs=[pl.BlockSpec(memory_space=pltpu.VMEM) for _ in column],
            out_specs=pl.BlockSpec((2, planes, ZG * 2, strip, side), lambda g, *_: (g, 0, 0, 0, 0)),
        ),
        name="pick_strips",
    )(wanted, *column)

    small = jnp.concatenate(
        [block_slots[:, None, :], block_windows // SUB, block_windows % SUB], axis=1
    ).reshape(planes, 1, 5 * blocks)
    small = jnp.pad(small, ((0, 0), (0, 3), (0, 128 - 5 * blocks)))
    cells = jnp.concatenate([fine_cells, long_cells], axis=1)
    ray_info = jnp.concatenate([cells, small], axis=2).astype(BF)
    arrived = [lax.dynamic_index_in_dim(ray_info, plane, 0, keepdims=False)]
    for d in range(1, planes):
        pairs = [(i, (i + d) % planes) for i in range(planes)]
        sent = lax.dynamic_index_in_dim(ray_info, (plane + d) % planes, 0, keepdims=False)
        arrived.append(lax.ppermute(sent, "planes", pairs))
    arrived = jnp.stack(arrived)
    outgoing, piece, arrived = lax.optimization_barrier((outgoing, piece, arrived))
    cells = arrived[:, :, :rays_here].astype(F32)
    small = arrived[:, 0, rays_here : rays_here + 5 * blocks].astype(jnp.int32)
    small = small.reshape(planes, 5, blocks)
    turn = (plane - jnp.arange(planes)) % planes
    small = jnp.sum(
        jnp.where(turn[:, None] == jnp.arange(planes), 1, 0)[:, :, None, None] * small[None], axis=1
    )
    slots = small[:, 0].reshape(planes * blocks)
    starts = (small[:, 1:3] * SUB + small[:, 3:5]).transpose(1, 0, 2).reshape(2, planes * blocks)
    whose = plane.reshape(1)

    incoming = lax.all_to_all(
        outgoing.reshape(level * planes, ZG * 2, strip, side),
        ("rays", "planes"),
        0,
        0,
        tiled=True,
        axis_index_groups=[
            list(range(z * level * planes, (z + 1) * level * planes)) for z in range(ZG)
        ],
    ).reshape(level, planes, ZG * 2, strip, side)

    distance = (my_z - owner // level) % ZG
    chosen = piece
    for d in range(1, ZG):
        chosen = jnp.where(distance == d, along_z(piece, d), chosen)

    my_list = lax.dynamic_slice(tile_lists, (my_row, plane, 0), (1, 1, list_len))[0, 0]
    my_owner = my_list // tile_dev
    place = jnp.arange(list_len, dtype=jnp.int32)
    repeat = (my_owner[:, None] == my_owner[None, :]) & (place[:, None] > place[None, :])
    rank = jnp.max(repeat.astype(jnp.int32), axis=1)
    entry = my_owner % level * (2 * ZG) + (my_z - my_owner // level) % ZG * 2 + rank

    chosen, incoming = lax.optimization_barrier((chosen, incoming))
    whole = exchange_flat(jnp.broadcast_to(chosen[None], (level, *chosen.shape)))
    whole = whole.reshape(2, extent, extent)

    smooth_table, slope_table = kernel_tables(side)
    left = jnp.concatenate([smooth_table, slope_table], axis=0)
    halves = 2
    wide = rays_here // halves
    vmem = pl.BlockSpec(memory_space=pltpu.VMEM)
    anywhere = pl.BlockSpec(memory_space=pl.ANY)
    params = pltpu.CompilerParams(vmem_limit_bytes=48 << 20)

    def cell_spec(h=None):
        def index(g, whose, *_):
            src = g if h is not None else g // halves
            return (whose[0] + planes - src) % planes, 0, h if h is not None else g % halves

        return pl.BlockSpec((1, 4, wide), index)

    fine_corners = pl.pallas_call(
        fine_kernel,
        out_shape=jax.ShapeDtypeStruct((planes, 8, rays_here), BF),
        grid_spec=pltpu.PrefetchScalarGridSpec(
            num_scalar_prefetch=3,
            grid=(planes * halves,),
            in_specs=[vmem, cell_spec(), vmem, vmem, vmem],
            out_specs=pl.BlockSpec((1, 8, wide), lambda g, *_: (g // halves, 0, g % halves)),
        ),
        compiler_params=params,
        name="fine_gather",
    )(whose, slots, entry, incoming, cells, left, with_next(slope_table), with_next(smooth_table))
    fine_corners, whole = lax.optimization_barrier((fine_corners, whole))
    fine_corners = lax.all_to_all(fine_corners, "planes", 0, 0, tiled=True)
    received = fine_corners
    outputs = (
        jax.ShapeDtypeStruct((planes, 2, rays_here), F32),
        jax.ShapeDtypeStruct((2, rays_here), F32),
    )
    results = ()
    part = 2048
    for h in range(halves):
        long_corners = pl.pallas_call(
            functools.partial(long_kernel, h, halves),
            out_shape=jax.ShapeDtypeStruct((planes, 8, wide), BF),
            grid_spec=pltpu.PrefetchScalarGridSpec(
                num_scalar_prefetch=2,
                grid=(planes,),
                in_specs=[vmem, cell_spec(h)],
                out_specs=pl.BlockSpec((1, 8, wide), lambda g, *_: (g, 0, 0)),
            ),
            compiler_params=params,
            name=f"long_gather_{h}",
        )(whose, starts, whole, cells)
        long_corners, whole, received = lax.optimization_barrier((long_corners, whole, received))
        received = lax.all_to_all(long_corners, "planes", 0, 0, tiled=True)
        steps = wide // part
        results = pl.pallas_call(
            functools.partial(final_kernel, len(results)),
            out_shape=outputs,
            grid=(steps,),
            in_specs=[
                pl.BlockSpec((planes, 8, part), lambda g, h=h: (0, 0, h * steps + g)),
                pl.BlockSpec((planes, 8, part), lambda g: (0, 0, g)),
                pl.BlockSpec((planes, 4, part), lambda g, h=h: (0, 0, h * steps + g)),
                *[anywhere for _ in results],
            ],
            out_specs=(
                pl.BlockSpec((planes, 2, part), lambda g, h=h: (0, 0, h * steps + g)),
                pl.BlockSpec((2, part), lambda g, h=h: (0, h * steps + g)),
            ),
            input_output_aliases={3 + i: i for i in range(len(results))},
            name=f"lens_sum_{h}",
        )(fine_corners, received, fractions, *results)
    return tuple(results)


def solution(mesh):
    return jax.shard_map(
        per_device,
        mesh=mesh,
        in_specs=(
            P(None, "rays", "planes", None),
            P("rays", None, None, None, None),
            P(),
            P(),
            P(None, ("rays", "planes")),
            P(None, None, ("rays", "planes")),
            P(None, None, ("rays", "planes")),
            P(None, None, ("rays", "planes")),
            P(None, None, ("rays", "planes")),
        ),
        out_specs=(P(None, None, ("rays", "planes")), P(None, ("rays", "planes"))),
        check_vma=False,
    )
```

```python
import functools

import jax
import jax.numpy as jnp
from jax import lax
from jax.experimental import pallas as pl
from jax.experimental.pallas import tpu as pltpu
from jax.sharding import PartitionSpec as P

RATIO = 16
BF = jnp.bfloat16
F32 = jnp.float32
SUB = 16
ZG = 4
TAPS = 6
HALF = 64


def kernel_tables(side):
    indices = jnp.arange(side, dtype=jnp.int32)
    offset = (indices[:, None] - indices[None, :]).astype(F32)
    tap_offsets = jnp.arange(-TAPS, TAPS + 1, dtype=jnp.int32).astype(F32)
    tap_total = jnp.sum(jnp.exp(-tap_offsets * tap_offsets / 8.0))
    inside = jnp.abs(offset) <= TAPS
    weight = jnp.where(inside, jnp.exp(-offset * offset / 8.0), 0.0) / tap_total
    smooth_table = weight.astype(BF)
    slope_table = (6.0 * offset * weight / 4.0).astype(BF)
    return (smooth_table, slope_table)


def with_next(table):
    following = jnp.concatenate([table[1:], jnp.zeros_like(table[:1])], axis=0)
    return jnp.concatenate([table.T, following.T], axis=1)


def onehot_tiles(row, tiles, width):
    wide = jnp.broadcast_to(row, (SUB, width)).astype(BF)
    place = lax.broadcasted_iota(jnp.int32, (SUB, width), 0).astype(F32)
    one = jnp.ones((SUB, width), BF)
    zero = jnp.zeros((SUB, width), BF)
    return [
        jnp.where(wide == (place + float(SUB * t)).astype(BF), one, zero) for t in range(tiles)
    ]


def two_halves(parts):
    return jnp.concatenate(
        [jnp.concatenate([p[: HALF + SUB], p[HALF:]], axis=1) for p in parts], axis=0
    )


def split_columns(row, column):
    upper = jnp.where(column >= float(HALF), 1.0, 0.0)
    return row + 2 * HALF * upper, column - HALF * upper


def corner_values(found, columns):
    rows, width = found.shape[0] // 4, found.shape[1]
    lane = 128
    half = 2 * lane
    results = []
    for h in range(width // half):
        lanes = slice(h * half, (h + 1) * half)
        column = columns[:, lanes]
        tile_of = [jnp.floor((column + step) * (1.0 / SUB)) for step in (0.0, 1.0)]
        wide = [jnp.broadcast_to(t, (SUB, half)).astype(BF) for t in tile_of]
        kept = [[None, None] for _ in range(4)]
        for t in range(rows // SUB):
            hit = [w == float(t) for w in wide]
            for i in range(4):
                low = found[i * rows + t * SUB : i * rows + (t + 1) * SUB, lanes].astype(BF)
                for s in range(2):
                    kept[i][s] = low if t == 0 else jnp.where(hit[s], low, kept[i][s])
        inner = [
            jnp.broadcast_to(column + s - SUB * tile_of[s], (8, half)).astype(jnp.int32)
            for s in range(2)
        ]
        for w in range(half // lane):
            cut = slice(w * lane, (w + 1) * lane)
            sub = lax.broadcasted_iota(jnp.int32, (8, lane), 0)
            value = None
            for s in range(2):
                row = inner[s][:, cut]
                upper, row = row >= 8, row & 7
                for i in range(4):
                    both = kept[i][s][:, cut].astype(F32)
                    one = jnp.where(upper, both[8:], both[:8])
                    one = jnp.take_along_axis(one, row, axis=0, mode="promise_in_bounds")
                    value = one if value is None else jnp.where(sub == 2 * i + s, one, value)
            results.append(value)
    return jnp.concatenate(results, axis=1)


def pipelined(count, stages):
    held = {}
    for turn in range(count + len(stages) - 1):
        for s, stage in enumerate(stages):
            item = turn - s
            if 0 <= item < count:
                held[item] = stage(item, held.get(item))


def fine_kernel(whose_ref, slot_ref, entry_ref, tiles_ref, cells_ref, left_ref, slope_ref, smooth_ref, out_ref):
    step = pl.program_id(0)
    width = 512
    per_step = out_ref.shape[2] // width
    places, strips = tiles_ref.shape[1:3]
    side = tiles_ref.shape[4]

    def lanes(b):
        return slice(b * width, (b + 1) * width)

    def columns_done(b):
        pair = []
        for i in (b, b + 1):
            entry = entry_ref[slot_ref[step * per_step + i]]
            source, place = entry // strips, entry % strips
            pair += [tiles_ref[source, k, place] for k in range(places)]
        return lax.dot_general(
            left_ref[...],
            jnp.concatenate(pair, axis=0),
            (((1,), (1,)), ((), ())),
            preferred_element_type=F32,
        ).astype(BF)

    def fields(partial):
        partial = [partial[:, :side], partial[:, side:]]
        along_x = jnp.concatenate([p[:side] for p in partial], axis=0)
        along_y = jnp.concatenate([p[side:] for p in partial], axis=0)
        along_x = jnp.dot(along_x, slope_ref[...], preferred_element_type=F32).astype(BF)
        along_y = jnp.dot(along_y, smooth_ref[...], preferred_element_type=F32).astype(BF)
        past = jnp.zeros((SUB, side), BF)
        tables = []
        for i in range(2):
            x, y = (a[i * side : (i + 1) * side] for a in (along_x, along_y))
            four = (x[:, :side], y[:, :side], x[:, side:], y[:, side:])
            tables.append(two_halves([jnp.concatenate([f, past], axis=0) for f in four]))
        return tables

    def gather_rows(b, table):
        row, _ = split_columns(cells_ref[0, 0:1, lanes(b)], cells_ref[0, 1:2, lanes(b)])
        hot = jnp.concatenate(onehot_tiles(row, 2 * side // SUB, width), axis=0)
        return jnp.dot(table, hot, preferred_element_type=F32)

    def gather_columns(b, found):
        _, column = split_columns(cells_ref[0, 0:1, lanes(b)], cells_ref[0, 1:2, lanes(b)])
        out_ref[0, :, lanes(b)] = corner_values(found, column).astype(BF)

    partial, tables, found = {}, {}, {}
    for turn in range(per_step + 4):
        if turn < per_step and turn % 2 == 0:
            partial[turn] = columns_done(turn)
        b = turn - 2
        if 0 <= b < per_step and b % 2 == 0:
            tables[b], tables[b + 1] = fields(partial.pop(b))
        b = turn - 3
        if 0 <= b < per_step:
            found[b] = gather_rows(b, tables.pop(b))
        b = turn - 4
        if 0 <= b < per_step:
            gather_columns(b, found.pop(b))


def long_kernel(part, parts, whose_ref, start_ref, map_ref, cells_ref, fine_ref, out_ref):
    step = pl.program_id(0)
    width = 512
    per_step = out_ref.shape[2] // width
    extent = map_ref.shape[1]
    side = 128
    rows = side + SUB

    def lanes(b):
        return slice(b * width, (b + 1) * width)

    def bases(b):
        block = (step * parts + part) * per_step + b
        row_start = start_ref[0, block]
        col_start = start_ref[1, block]
        row_base = jnp.minimum(row_start // side, extent // side - 2) * side
        col_base = jnp.minimum(col_start // SUB, (extent - rows) // SUB) * SUB
        return row_start, pl.multiple_of(row_base, side), col_start, pl.multiple_of(col_base, SUB)

    def place(b):
        _, _, col_start, col_base = bases(b)
        column = cells_ref[0, 3:4, lanes(b)] + (col_start - col_base).astype(F32)
        return split_columns(cells_ref[0, 2:3, lanes(b)], column)

    def gather_rows(b, _):
        row_start, row_base, _, col_base = bases(b)
        offset = row_start - row_base
        parts = []
        for turn in ((2 * side - offset) & (2 * side - 1), 2 * side - 1 - offset):
            for i in range(2):
                window = map_ref[i, pl.ds(col_base, rows), pl.ds(row_base, 2 * side)]
                parts.append(pltpu.roll(window, turn, axis=1)[:, :side])
        row, _ = place(b)
        hot = jnp.concatenate(onehot_tiles(row, 2 * side // SUB, width), axis=0)
        return jnp.dot(two_halves(parts), hot, preferred_element_type=F32)

    def gather_columns(b, found):
        _, column = place(b)
        both = (fine_ref[0, :, lanes(b)].astype(F32), corner_values(found, column))
        out_ref[0, :, lanes(b)] = jnp.concatenate(both, axis=0).astype(BF)

    pipelined(per_step, (gather_rows, gather_columns))


def pick_kernel(wanted_ref, *refs):
    sources, out_ref = refs[:-1], refs[-1]
    step = pl.program_id(0)
    count, planes, places = out_ref.shape[:3]
    each = places // len(sources)
    for i in range(count):
        for k in range(planes):
            for j in range(places):
                tile = wanted_ref[step * count + i, k * places + j]
                out_ref[i, k, j] = sources[j // each][k, tile]


def weighted(corners, p, q):
    sub = lax.broadcasted_iota(jnp.int32, corners.shape, 0)
    p, q = jnp.broadcast_to(p, corners.shape), jnp.broadcast_to(q, corners.shape)
    row = jnp.where(sub < 4, 1.0 - p, p).astype(BF).astype(F32)
    column = jnp.where(sub % 2 == 0, 1.0 - q, q)
    return corners * row * column


def lens_shift(previous, target):
    shift = 0.0
    for earlier, deflection in enumerate(previous):
        shift = shift - (target - earlier) / target * deflection
    return shift


def final_kernel(held, corners_ref, frac_ref, *refs):
    deflection_ref, source_ref = refs[held:]
    planes, part = corners_ref.shape[0], frac_ref.shape[2]
    lanes = pl.ds(pl.multiple_of(pl.program_id(0) * part, part), part)
    found = []
    for k in range(planes):
        at = frac_ref[k]
        p, q, p2, q2 = (at[i : i + 1] for i in range(4))
        if k > 0:
            shift = lens_shift(found, k)
            sx, sy = shift[0:1], shift[2:3]
            p, q, p2, q2 = p + sx, q + sy, p2 + sx / RATIO, q2 + sy / RATIO
        corners = corners_ref[k, :, lanes].astype(F32)
        terms = weighted(corners[:8], p, q) + weighted(corners[8:], p2, q2)
        terms = terms + pltpu.roll(terms, 4, axis=0)
        terms = terms + pltpu.roll(terms, 7, axis=0)
        found.append(terms)
        deflection_ref[k, 0:1] = terms[0:1]
        deflection_ref[k, 1:2] = terms[2:3]
    shift = lens_shift(found, planes)
    source_ref[0:1] = shift[0:1]
    source_ref[1:2] = shift[2:3]


def per_device(
    tile_density,
    long_maps,
    map_owner,
    tile_lists,
    block_slots,
    block_windows,
    fine_cells,
    long_cells,
    fractions,
):
    my_row = lax.axis_index("rays")
    plane = lax.axis_index("planes")
    planes, tile_dev, strip, side = tile_density.shape
    extent = long_maps.shape[2]
    list_len = tile_lists.shape[2]
    rays_here = fine_cells.shape[2]
    blocks = block_slots.shape[1]
    ray_count = lax.axis_size("rays")
    level = ray_count // ZG
    my_z, my_xy = my_row // level, my_row % level
    flat_groups = [[z * level + i for i in range(level)] for z in range(ZG)]

    def moved(x, stride, d):
        pairs = [(r, r + ((r // stride + d) % ZG - r // stride % ZG) * stride) for r in range(ray_count)]
        return lax.ppermute(x, "rays", pairs)

    def along_z(x, d):
        return moved(x, level, d)

    def exchange_flat(x):
        return lax.all_to_all(x, "rays", 0, 0, tiled=True, axis_index_groups=flat_groups)

    column = [tile_density] + [along_z(tile_density, d) for d in range(1, ZG)]

    own_map = lax.dynamic_index_in_dim(long_maps[0], plane, 0, keepdims=False)
    own_map = own_map.transpose(1, 2, 0).reshape(level, 2 * extent // level, extent)
    owner = lax.dynamic_index_in_dim(map_owner, plane, 0, keepdims=False)
    pieces = exchange_flat(own_map)
    piece = lax.dynamic_index_in_dim(pieces, owner % level, 0, keepdims=False)

    level_lists = lax.dynamic_slice(tile_lists, (my_z * level, 0, 0), (level, planes, list_len))
    owners = level_lists // tile_dev
    key = jnp.arange(list_len, dtype=jnp.int32) * tile_dev + level_lists % tile_dev
    column_owner = (my_z - jnp.arange(ZG, dtype=jnp.int32)) % ZG * level + my_xy
    mine = owners[:, :, None, :] == column_owner[None, None, :, None]
    first = jnp.min(jnp.where(mine, key[:, :, None, :], tile_dev * list_len), axis=3) % tile_dev
    last = jnp.max(jnp.where(mine, key[:, :, None, :], 0), axis=3) % tile_dev
    wanted = jnp.stack([first, last], axis=3).reshape(level, planes * ZG * 2)
    outgoing = pl.pallas_call(
        pick_kernel,
        out_shape=jax.ShapeDtypeStruct((level, planes, ZG * 2, strip, side), BF),
        grid_spec=pltpu.PrefetchScalarGridSpec(
            num_scalar_prefetch=1,
            grid=(level // 2,),
            in_specs=[pl.BlockSpec(memory_space=pltpu.VMEM) for _ in column],
            out_specs=pl.BlockSpec((2, planes, ZG * 2, strip, side), lambda g, *_: (g, 0, 0, 0, 0)),
        ),
        name="pick_strips",
    )(wanted, *column)

    small = jnp.concatenate(
        [block_slots[:, None, :], block_windows // SUB, block_windows % SUB], axis=1
    ).reshape(planes, 1, 5 * blocks)
    small = jnp.pad(small, ((0, 0), (0, 3), (0, 128 - 5 * blocks)))
    cells = jnp.concatenate([fine_cells, long_cells], axis=1)
    ray_info = jnp.concatenate([cells, small], axis=2).astype(BF)
    arrived = [lax.dynamic_index_in_dim(ray_info, plane, 0, keepdims=False)]
    for d in range(1, planes):
        pairs = [(i, (i + d) % planes) for i in range(planes)]
        sent = lax.dynamic_index_in_dim(ray_info, (plane + d) % planes, 0, keepdims=False)
        arrived.append(lax.ppermute(sent, "planes", pairs))
    arrived = jnp.stack(arrived)
    outgoing, piece, arrived = lax.optimization_barrier((outgoing, piece, arrived))
    cells = arrived[:, :, :rays_here].astype(F32)
    small = arrived[:, 0, rays_here : rays_here + 5 * blocks].astype(jnp.int32)
    small = small.reshape(planes, 5, blocks)
    turn = (plane - jnp.arange(planes)) % planes
    small = jnp.sum(
        jnp.where(turn[:, None] == jnp.arange(planes), 1, 0)[:, :, None, None] * small[None], axis=1
    )
    slots = small[:, 0].reshape(planes * blocks)
    starts = (small[:, 1:3] * SUB + small[:, 3:5]).transpose(1, 0, 2).reshape(2, planes * blocks)
    whose = plane.reshape(1)

    incoming = lax.all_to_all(
        outgoing.reshape(level * planes, ZG * 2, strip, side),
        ("rays", "planes"),
        0,
        0,
        tiled=True,
        axis_index_groups=[
            list(range(z * level * planes, (z + 1) * level * planes)) for z in range(ZG)
        ],
    ).reshape(level, planes, ZG * 2, strip, side)

    distance = (my_z - owner // level) % ZG
    chosen = piece
    for d in range(1, ZG):
        chosen = jnp.where(distance == d, along_z(piece, d), chosen)

    my_list = lax.dynamic_slice(tile_lists, (my_row, plane, 0), (1, 1, list_len))[0, 0]
    my_owner = my_list // tile_dev
    place = jnp.arange(list_len, dtype=jnp.int32)
    repeat = (my_owner[:, None] == my_owner[None, :]) & (place[:, None] > place[None, :])
    rank = jnp.max(repeat.astype(jnp.int32), axis=1)
    entry = my_owner % level * (2 * ZG) + (my_z - my_owner // level) % ZG * 2 + rank

    copies = jnp.broadcast_to(chosen[None], (level, *chosen.shape))
    copies, incoming = lax.optimization_barrier((copies, incoming))
    whole = exchange_flat(copies)
    whole = whole.reshape(2, extent, extent)

    smooth_table, slope_table = kernel_tables(side)
    left = jnp.concatenate([smooth_table, slope_table], axis=0)
    halves = 2
    wide = rays_here // halves
    vmem = pl.BlockSpec(memory_space=pltpu.VMEM)
    anywhere = pl.BlockSpec(memory_space=pl.ANY)
    params = pltpu.CompilerParams(vmem_limit_bytes=48 << 20)

    def cell_spec(h=None):
        def index(g, whose, *_):
            src = g if h is not None else g // halves
            return (whose[0] + planes - src) % planes, 0, h if h is not None else g % halves

        return pl.BlockSpec((1, 4, wide), index)

    fine_corners = pl.pallas_call(
        fine_kernel,
        out_shape=jax.ShapeDtypeStruct((planes, 8, rays_here), BF),
        grid_spec=pltpu.PrefetchScalarGridSpec(
            num_scalar_prefetch=3,
            grid=(planes * halves,),
            in_specs=[vmem, cell_spec(), vmem, vmem, vmem],
            out_specs=pl.BlockSpec((1, 8, wide), lambda g, *_: (g // halves, 0, g % halves)),
        ),
        compiler_params=params,
        name="fine_gather",
    )(whose, slots, entry, incoming, cells, left, with_next(slope_table), with_next(smooth_table))
    outputs = (
        jax.ShapeDtypeStruct((planes, 2, rays_here), F32),
        jax.ShapeDtypeStruct((2, rays_here), F32),
    )
    results, returned = (), []
    part = 2048
    for h in range(halves):
        corners = pl.pallas_call(
            functools.partial(long_kernel, h, halves),
            out_shape=jax.ShapeDtypeStruct((planes, 16, wide), BF),
            grid_spec=pltpu.PrefetchScalarGridSpec(
                num_scalar_prefetch=2,
                grid=(planes,),
                in_specs=[
                    vmem,
                    cell_spec(h),
                    pl.BlockSpec((1, 8, wide), lambda g, *_, h=h: (g, 0, h)),
                ],
                out_specs=pl.BlockSpec((1, 16, wide), lambda g, *_: (g, 0, 0)),
            ),
            compiler_params=params,
            name=f"long_gather_{h}",
        )(whose, starts, whole, cells, fine_corners)
        if h > 0:
            corners, received = lax.optimization_barrier((corners, received))
        elif halves > 1:
            corners, whole = lax.optimization_barrier((corners, whole))
        received = lax.all_to_all(corners, "planes", 0, 0, tiled=True)
        returned.append(received)
    steps = wide // part
    for h in range(halves):
        results = pl.pallas_call(
            functools.partial(final_kernel, len(results)),
            out_shape=outputs,
            grid=(steps,),
            in_specs=[
                vmem,
                pl.BlockSpec((planes, 4, part), lambda g, h=h: (0, 0, h * steps + g)),
                *[anywhere for _ in results],
            ],
            out_specs=(
                pl.BlockSpec((planes, 2, part), lambda g, h=h: (0, 0, h * steps + g)),
                pl.BlockSpec((2, part), lambda g, h=h: (0, h * steps + g)),
            ),
            input_output_aliases={2 + i: i for i in range(len(results))},
            name=f"lens_sum_{h}",
        )(returned[h], fractions, *results)
    return tuple(results)


def solution(mesh):
    return jax.shard_map(
        per_device,
        mesh=mesh,
        in_specs=(
            P(None, "rays", "planes", None),
            P("rays", None, None, None, None),
            P(),
            P(),
            P(None, ("rays", "planes")),
            P(None, None, ("rays", "planes")),
            P(None, None, ("rays", "planes")),
            P(None, None, ("rays", "planes")),
            P(None, None, ("rays", "planes")),
        ),
        out_specs=(P(None, None, ("rays", "planes")), P(None, ("rays", "planes"))),
        check_vma=False,
    )
```

```python
import jax
import jax.numpy as jnp
from jax import lax
from jax.experimental import pallas as pl
from jax.experimental.pallas import tpu as pltpu
from jax.sharding import PartitionSpec as P

RATIO = 16
BF = jnp.bfloat16
F32 = jnp.float32
SUB = 16
ZG = 4
TAPS = 6
HALF = 64


def kernel_tables(side):
    indices = jnp.arange(side, dtype=jnp.int32)
    offset = (indices[:, None] - indices[None, :]).astype(F32)
    tap_offsets = jnp.arange(-TAPS, TAPS + 1, dtype=jnp.int32).astype(F32)
    tap_total = jnp.sum(jnp.exp(-tap_offsets * tap_offsets / 8.0))
    inside = jnp.abs(offset) <= TAPS
    weight = jnp.where(inside, jnp.exp(-offset * offset / 8.0), 0.0) / tap_total
    smooth_table = weight.astype(BF)
    slope_table = (6.0 * offset * weight / 4.0).astype(BF)
    return (smooth_table, slope_table)


def with_next(table):
    following = jnp.concatenate([table[1:], jnp.zeros_like(table[:1])], axis=0)
    return jnp.concatenate([table.T, following.T], axis=1)


def onehot_tiles(row, tiles, width):
    wide = jnp.broadcast_to(row, (SUB, width)).astype(BF)
    place = lax.broadcasted_iota(jnp.int32, (SUB, width), 0).astype(F32)
    one = jnp.ones((SUB, width), BF)
    zero = jnp.zeros((SUB, width), BF)
    return [
        jnp.where(wide == (place + float(SUB * t)).astype(BF), one, zero) for t in range(tiles)
    ]


def two_halves(parts):
    return jnp.concatenate(
        [jnp.concatenate([p[: HALF + SUB], p[HALF:]], axis=1) for p in parts], axis=0
    )


def split_columns(row, column):
    upper = jnp.where(column >= float(HALF), 1.0, 0.0)
    return row + 2 * HALF * upper, column - HALF * upper


def corner_values(found, columns):
    rows, width = found.shape[0] // 4, found.shape[1]
    lane = 128
    half = 2 * lane
    results = []
    for h in range(width // half):
        lanes = slice(h * half, (h + 1) * half)
        column = columns[:, lanes]
        tile_of = [jnp.floor((column + step) * (1.0 / SUB)) for step in (0.0, 1.0)]
        wide = [jnp.broadcast_to(t, (SUB, half)).astype(BF) for t in tile_of]
        kept = [[None, None] for _ in range(4)]
        for t in range(rows // SUB):
            hit = [w == float(t) for w in wide]
            for i in range(4):
                low = found[i * rows + t * SUB : i * rows + (t + 1) * SUB, lanes].astype(BF)
                for s in range(2):
                    kept[i][s] = low if t == 0 else jnp.where(hit[s], low, kept[i][s])
        inner = [
            jnp.broadcast_to(column + s - SUB * tile_of[s], (8, half)).astype(jnp.int32)
            for s in range(2)
        ]
        for w in range(half // lane):
            cut = slice(w * lane, (w + 1) * lane)
            sub = lax.broadcasted_iota(jnp.int32, (8, lane), 0)
            value = None
            for s in range(2):
                row = inner[s][:, cut]
                upper, row = row >= 8, row & 7
                for i in range(4):
                    both = kept[i][s][:, cut].astype(F32)
                    one = jnp.where(upper, both[8:], both[:8])
                    one = jnp.take_along_axis(one, row, axis=0, mode="promise_in_bounds")
                    value = one if value is None else jnp.where(sub == 2 * i + s, one, value)
            results.append(value)
    return jnp.concatenate(results, axis=1)


def pipelined(count, stages):
    held = {}
    for turn in range(count + len(stages) - 1):
        for s, stage in enumerate(stages):
            item = turn - s
            if 0 <= item < count:
                held[item] = stage(item, held.get(item))


def fine_kernel(whose_ref, slot_ref, entry_ref, tiles_ref, cells_ref, left_ref, slope_ref, smooth_ref, out_ref):
    step = pl.program_id(0)
    width = 512
    per_step = out_ref.shape[2] // width
    places, strips = tiles_ref.shape[1:3]
    side = tiles_ref.shape[4]

    def lanes(b):
        return slice(b * width, (b + 1) * width)

    def columns_done(b):
        pair = []
        for i in (b, b + 1):
            entry = entry_ref[slot_ref[step * per_step + i]]
            source, place = entry // strips, entry % strips
            pair += [tiles_ref[source, k, place] for k in range(places)]
        return lax.dot_general(
            left_ref[...],
            jnp.concatenate(pair, axis=0),
            (((1,), (1,)), ((), ())),
            preferred_element_type=F32,
        ).astype(BF)

    def fields(partial):
        partial = [partial[:, :side], partial[:, side:]]
        along_x = jnp.concatenate([p[:side] for p in partial], axis=0)
        along_y = jnp.concatenate([p[side:] for p in partial], axis=0)
        along_x = jnp.dot(along_x, slope_ref[...], preferred_element_type=F32).astype(BF)
        along_y = jnp.dot(along_y, smooth_ref[...], preferred_element_type=F32).astype(BF)
        past = jnp.zeros((SUB, side), BF)
        tables = []
        for i in range(2):
            x, y = (a[i * side : (i + 1) * side] for a in (along_x, along_y))
            four = (x[:, :side], y[:, :side], x[:, side:], y[:, side:])
            tables.append(two_halves([jnp.concatenate([f, past], axis=0) for f in four]))
        return tables

    def gather_rows(b, table):
        row, _ = split_columns(cells_ref[0, 0:1, lanes(b)], cells_ref[0, 1:2, lanes(b)])
        hot = jnp.concatenate(onehot_tiles(row, 2 * side // SUB, width), axis=0)
        return jnp.dot(table, hot, preferred_element_type=F32)

    def gather_columns(b, found):
        _, column = split_columns(cells_ref[0, 0:1, lanes(b)], cells_ref[0, 1:2, lanes(b)])
        out_ref[0, :, lanes(b)] = corner_values(found, column).astype(BF)

    partial, tables, found = {}, {}, {}
    for turn in range(per_step + 4):
        if turn < per_step and turn % 2 == 0:
            partial[turn] = columns_done(turn)
        b = turn - 2
        if 0 <= b < per_step and b % 2 == 0:
            tables[b], tables[b + 1] = fields(partial.pop(b))
        b = turn - 3
        if 0 <= b < per_step:
            found[b] = gather_rows(b, tables.pop(b))
        b = turn - 4
        if 0 <= b < per_step:
            gather_columns(b, found.pop(b))


def long_kernel(whose_ref, start_ref, map_ref, cells_ref, fine_ref, out_ref):
    step = pl.program_id(0)
    width = 512
    per_step = out_ref.shape[2] // width
    extent = map_ref.shape[1]
    side = 128
    rows = side + SUB

    def lanes(b):
        return slice(b * width, (b + 1) * width)

    def bases(b):
        block = step * per_step + b
        row_start = start_ref[0, block]
        col_start = start_ref[1, block]
        row_base = jnp.minimum(row_start // side, extent // side - 2) * side
        col_base = jnp.minimum(col_start // SUB, (extent - rows) // SUB) * SUB
        return row_start, pl.multiple_of(row_base, side), col_start, pl.multiple_of(col_base, SUB)

    def place(b):
        _, _, col_start, col_base = bases(b)
        column = cells_ref[0, 3:4, lanes(b)] + (col_start - col_base).astype(F32)
        return split_columns(cells_ref[0, 2:3, lanes(b)], column)

    def gather_rows(b, _):
        row_start, row_base, _, col_base = bases(b)
        offset = row_start - row_base
        parts = []
        for turn in ((2 * side - offset) & (2 * side - 1), 2 * side - 1 - offset):
            for i in range(2):
                window = map_ref[i, pl.ds(col_base, rows), pl.ds(row_base, 2 * side)]
                parts.append(pltpu.roll(window, turn, axis=1)[:, :side])
        row, _ = place(b)
        hot = jnp.concatenate(onehot_tiles(row, 2 * side // SUB, width), axis=0)
        return jnp.dot(two_halves(parts), hot, preferred_element_type=F32)

    def gather_columns(b, found):
        _, column = place(b)
        both = (fine_ref[0, :, lanes(b)].astype(F32), corner_values(found, column))
        out_ref[0, :, lanes(b)] = jnp.concatenate(both, axis=0).astype(BF)

    pipelined(per_step, (gather_rows, gather_columns))


def pick_kernel(wanted_ref, *refs):
    sources, out_ref = refs[:-1], refs[-1]
    step = pl.program_id(0)
    count, planes, places = out_ref.shape[:3]
    each = places // len(sources)
    for i in range(count):
        for k in range(planes):
            for j in range(places):
                tile = wanted_ref[step * count + i, k * places + j]
                out_ref[i, k, j] = sources[j // each][k, tile]


def weighted(corners, p, q):
    sub = lax.broadcasted_iota(jnp.int32, corners.shape, 0)
    p, q = jnp.broadcast_to(p, corners.shape), jnp.broadcast_to(q, corners.shape)
    row = jnp.where(sub < 4, 1.0 - p, p).astype(BF).astype(F32)
    column = jnp.where(sub % 2 == 0, 1.0 - q, q)
    return corners * row * column


def lens_shift(previous, target):
    shift = 0.0
    for earlier, deflection in enumerate(previous):
        shift = shift - (target - earlier) / target * deflection
    return shift


def final_kernel(corners_ref, frac_ref, deflection_ref, source_ref):
    planes = corners_ref.shape[0]
    found = []
    for k in range(planes):
        at = frac_ref[k]
        p, q, p2, q2 = (at[i : i + 1] for i in range(4))
        if k > 0:
            shift = lens_shift(found, k)
            sx, sy = shift[0:1], shift[2:3]
            p, q, p2, q2 = p + sx, q + sy, p2 + sx / RATIO, q2 + sy / RATIO
        corners = corners_ref[k].astype(F32)
        terms = weighted(corners[:8], p, q) + weighted(corners[8:], p2, q2)
        terms = terms + pltpu.roll(terms, 4, axis=0)
        terms = terms + pltpu.roll(terms, 7, axis=0)
        found.append(terms)
        deflection_ref[k, 0:1] = terms[0:1]
        deflection_ref[k, 1:2] = terms[2:3]
    shift = lens_shift(found, planes)
    source_ref[0:1] = shift[0:1]
    source_ref[1:2] = shift[2:3]


def per_device(
    tile_density,
    long_maps,
    map_owner,
    tile_lists,
    block_slots,
    block_windows,
    fine_cells,
    long_cells,
    fractions,
):
    my_row = lax.axis_index("rays")
    plane = lax.axis_index("planes")
    planes, tile_dev, strip, side = tile_density.shape
    extent = long_maps.shape[2]
    list_len = tile_lists.shape[2]
    rays_here = fine_cells.shape[2]
    blocks = block_slots.shape[1]
    ray_count = lax.axis_size("rays")
    level = ray_count // ZG
    my_z, my_xy = my_row // level, my_row % level
    flat_groups = [[z * level + i for i in range(level)] for z in range(ZG)]

    def moved(x, stride, d):
        pairs = [(r, r + ((r // stride + d) % ZG - r // stride % ZG) * stride) for r in range(ray_count)]
        return lax.ppermute(x, "rays", pairs)

    def along_z(x, d):
        return moved(x, level, d)

    def exchange_flat(x):
        return lax.all_to_all(x, "rays", 0, 0, tiled=True, axis_index_groups=flat_groups)

    column = [tile_density] + [along_z(tile_density, d) for d in range(1, ZG)]

    own_map = lax.dynamic_index_in_dim(long_maps[0], plane, 0, keepdims=False)
    own_map = own_map.transpose(1, 2, 0).reshape(level, 2 * extent // level, extent)
    owner = lax.dynamic_index_in_dim(map_owner, plane, 0, keepdims=False)
    pieces = exchange_flat(own_map)
    piece = lax.dynamic_index_in_dim(pieces, owner % level, 0, keepdims=False)

    level_lists = lax.dynamic_slice(tile_lists, (my_z * level, 0, 0), (level, planes, list_len))
    owners = level_lists // tile_dev
    key = jnp.arange(list_len, dtype=jnp.int32) * tile_dev + level_lists % tile_dev
    column_owner = (my_z - jnp.arange(ZG, dtype=jnp.int32)) % ZG * level + my_xy
    mine = owners[:, :, None, :] == column_owner[None, None, :, None]
    first = jnp.min(jnp.where(mine, key[:, :, None, :], tile_dev * list_len), axis=3) % tile_dev
    last = jnp.max(jnp.where(mine, key[:, :, None, :], 0), axis=3) % tile_dev
    wanted = jnp.stack([first, last], axis=3).reshape(level, planes * ZG * 2)
    outgoing = pl.pallas_call(
        pick_kernel,
        out_shape=jax.ShapeDtypeStruct((level, planes, ZG * 2, strip, side), BF),
        grid_spec=pltpu.PrefetchScalarGridSpec(
            num_scalar_prefetch=1,
            grid=(level // 2,),
            in_specs=[pl.BlockSpec(memory_space=pltpu.VMEM) for _ in column],
            out_specs=pl.BlockSpec((2, planes, ZG * 2, strip, side), lambda g, *_: (g, 0, 0, 0, 0)),
        ),
        name="pick_strips",
    )(wanted, *column)

    block_slots, block_windows, fine_cells, long_cells, _ = lax.optimization_barrier(
        (block_slots, block_windows, fine_cells, long_cells, own_map)
    )
    small = jnp.concatenate(
        [block_slots[:, None, :], block_windows // SUB, block_windows % SUB], axis=1
    ).reshape(planes, 1, 5 * blocks)
    small = jnp.pad(small, ((0, 0), (0, 3), (0, 128 - 5 * blocks)))
    cells = jnp.concatenate([fine_cells, long_cells], axis=1)
    ray_info = jnp.concatenate([cells, small], axis=2).astype(BF)
    arrived = [lax.dynamic_index_in_dim(ray_info, plane, 0, keepdims=False)]
    for d in range(1, planes):
        pairs = [(i, (i + d) % planes) for i in range(planes)]
        sent = lax.dynamic_index_in_dim(ray_info, (plane + d) % planes, 0, keepdims=False)
        arrived.append(lax.ppermute(sent, "planes", pairs))
    arrived = jnp.stack(arrived)
    outgoing, piece, arrived = lax.optimization_barrier((outgoing, piece, arrived))
    cells = arrived[:, :, :rays_here].astype(F32)
    small = arrived[:, 0, rays_here : rays_here + 5 * blocks].astype(jnp.int32)
    small = small.reshape(planes, 5, blocks)
    turn = (plane - jnp.arange(planes)) % planes
    small = jnp.sum(
        jnp.where(turn[:, None] == jnp.arange(planes), 1, 0)[:, :, None, None] * small[None], axis=1
    )
    slots = small[:, 0].reshape(planes * blocks)
    starts = (small[:, 1:3] * SUB + small[:, 3:5]).transpose(1, 0, 2).reshape(2, planes * blocks)
    whose = plane.reshape(1)

    incoming = lax.all_to_all(
        outgoing.reshape(level * planes, ZG * 2, strip, side),
        ("rays", "planes"),
        0,
        0,
        tiled=True,
        axis_index_groups=[
            list(range(z * level * planes, (z + 1) * level * planes)) for z in range(ZG)
        ],
    ).reshape(level, planes, ZG * 2, strip, side)

    distance = (my_z - owner // level) % ZG
    chosen = piece
    for d in range(1, ZG):
        chosen = jnp.where(distance == d, along_z(piece, d), chosen)

    my_list = lax.dynamic_slice(tile_lists, (my_row, plane, 0), (1, 1, list_len))[0, 0]
    my_owner = my_list // tile_dev
    place = jnp.arange(list_len, dtype=jnp.int32)
    repeat = (my_owner[:, None] == my_owner[None, :]) & (place[:, None] > place[None, :])
    rank = jnp.max(repeat.astype(jnp.int32), axis=1)
    entry = my_owner % level * (2 * ZG) + (my_z - my_owner // level) % ZG * 2 + rank

    copies = jnp.broadcast_to(chosen[None], (level, *chosen.shape))
    copies, incoming = lax.optimization_barrier((copies, incoming))
    whole = exchange_flat(copies)
    whole = whole.reshape(2, extent, extent)

    smooth_table, slope_table = kernel_tables(side)
    left = jnp.concatenate([smooth_table, slope_table], axis=0)
    halves = 2
    wide = rays_here // halves
    vmem = pl.BlockSpec(memory_space=pltpu.VMEM)
    params = pltpu.CompilerParams(vmem_limit_bytes=48 << 20)

    def cell_spec():
        return pl.BlockSpec(
            (1, 4, wide),
            lambda g, whose, *_: ((whose[0] + planes - g // halves) % planes, 0, g % halves),
        )

    fine_corners = pl.pallas_call(
        fine_kernel,
        out_shape=jax.ShapeDtypeStruct((planes, 8, rays_here), BF),
        grid_spec=pltpu.PrefetchScalarGridSpec(
            num_scalar_prefetch=3,
            grid=(planes * halves,),
            in_specs=[vmem, cell_spec(), vmem, vmem, vmem],
            out_specs=pl.BlockSpec((1, 8, wide), lambda g, *_: (g // halves, 0, g % halves)),
        ),
        compiler_params=params,
        name="fine_gather",
    )(whose, slots, entry, incoming, cells, left, with_next(slope_table), with_next(smooth_table))
    corners = pl.pallas_call(
        long_kernel,
        out_shape=jax.ShapeDtypeStruct((planes, 16, rays_here), BF),
        grid_spec=pltpu.PrefetchScalarGridSpec(
            num_scalar_prefetch=2,
            grid=(planes * halves,),
            in_specs=[
                vmem,
                cell_spec(),
                pl.BlockSpec((1, 8, wide), lambda g, *_: (g // halves, 0, g % halves)),
            ],
            out_specs=pl.BlockSpec((1, 16, wide), lambda g, *_: (g // halves, 0, g % halves)),
        ),
        compiler_params=params,
        name="long_gather",
    )(whose, starts, whole, cells, fine_corners)
    corners = lax.all_to_all(corners, "planes", 0, 0, tiled=True)
    part = 2048
    return tuple(
        pl.pallas_call(
            final_kernel,
            out_shape=(
                jax.ShapeDtypeStruct((planes, 2, rays_here), F32),
                jax.ShapeDtypeStruct((2, rays_here), F32),
            ),
            grid=(rays_here // part,),
            in_specs=[
                pl.BlockSpec((planes, 16, part), lambda g: (0, 0, g)),
                pl.BlockSpec((planes, 4, part), lambda g: (0, 0, g)),
            ],
            out_specs=(
                pl.BlockSpec((planes, 2, part), lambda g: (0, 0, g)),
                pl.BlockSpec((2, part), lambda g: (0, g)),
            ),
            name="lens_sum",
        )(corners, fractions)
    )


def solution(mesh):
    return jax.shard_map(
        per_device,
        mesh=mesh,
        in_specs=(
            P(None, "rays", "planes", None),
            P("rays", None, None, None, None),
            P(),
            P(),
            P(None, ("rays", "planes")),
            P(None, None, ("rays", "planes")),
            P(None, None, ("rays", "planes")),
            P(None, None, ("rays", "planes")),
            P(None, None, ("rays", "planes")),
        ),
        out_specs=(P(None, None, ("rays", "planes")), P(None, ("rays", "planes"))),
        check_vma=False,
    )
```

```python
import jax
import jax.numpy as jnp
from jax import lax
from jax.experimental import pallas as pl
from jax.experimental.pallas import tpu as pltpu
from jax.sharding import PartitionSpec as P

RATIO = 16
BF = jnp.bfloat16
F32 = jnp.float32
SUB = 16
ZG = 4
TAPS = 6
HALF = 64


def kernel_tables(side):
    indices = jnp.arange(side, dtype=jnp.int32)
    offset = (indices[:, None] - indices[None, :]).astype(F32)
    tap_offsets = jnp.arange(-TAPS, TAPS + 1, dtype=jnp.int32).astype(F32)
    tap_total = jnp.sum(jnp.exp(-tap_offsets * tap_offsets / 8.0))
    inside = jnp.abs(offset) <= TAPS
    weight = jnp.where(inside, jnp.exp(-offset * offset / 8.0), 0.0) / tap_total
    smooth_table = weight.astype(BF)
    slope_table = (6.0 * offset * weight / 4.0).astype(BF)
    return (smooth_table, slope_table)


def with_next(table):
    following = jnp.concatenate([table[1:], jnp.zeros_like(table[:1])], axis=0)
    return jnp.concatenate([table.T, following.T], axis=1)


def onehot_tiles(row, tiles, width):
    wide = jnp.broadcast_to(row, (SUB, width)).astype(BF)
    place = lax.broadcasted_iota(jnp.int32, (SUB, width), 0).astype(F32)
    one = jnp.ones((SUB, width), BF)
    zero = jnp.zeros((SUB, width), BF)
    return [
        jnp.where(wide == (place + float(SUB * t)).astype(BF), one, zero) for t in range(tiles)
    ]


def two_halves(parts):
    return jnp.concatenate(
        [jnp.concatenate([p[: HALF + SUB], p[HALF:]], axis=1) for p in parts], axis=0
    )


def split_columns(row, column):
    upper = jnp.where(column >= float(HALF), 1.0, 0.0)
    return row + 2 * HALF * upper, column - HALF * upper


def corner_values(found, columns):
    rows, width = found.shape[0] // 4, found.shape[1]
    lane = 128
    half = 2 * lane
    results = []
    for h in range(width // half):
        lanes = slice(h * half, (h + 1) * half)
        column = columns[:, lanes]
        tile_of = [jnp.floor((column + step) * (1.0 / SUB)) for step in (0.0, 1.0)]
        wide = [jnp.broadcast_to(t, (SUB, half)).astype(BF) for t in tile_of]
        kept = [[None, None] for _ in range(4)]
        for t in range(rows // SUB):
            hit = [w == float(t) for w in wide]
            for i in range(4):
                low = found[i * rows + t * SUB : i * rows + (t + 1) * SUB, lanes].astype(BF)
                for s in range(2):
                    kept[i][s] = low if t == 0 else jnp.where(hit[s], low, kept[i][s])
        inner = [
            jnp.broadcast_to(column + s - SUB * tile_of[s], (8, half)).astype(jnp.int32)
            for s in range(2)
        ]
        for w in range(half // lane):
            cut = slice(w * lane, (w + 1) * lane)
            sub = lax.broadcasted_iota(jnp.int32, (8, lane), 0)
            value = None
            for s in range(2):
                row = inner[s][:, cut]
                upper, row = row >= 8, row & 7
                for i in range(4):
                    both = kept[i][s][:, cut].astype(F32)
                    one = jnp.where(upper, both[8:], both[:8])
                    one = jnp.take_along_axis(one, row, axis=0, mode="promise_in_bounds")
                    value = one if value is None else jnp.where(sub == 2 * i + s, one, value)
            results.append(value)
    return jnp.concatenate(results, axis=1)


def pipelined(count, stages):
    held = {}
    for turn in range(count + len(stages) - 1):
        for s, stage in enumerate(stages):
            item = turn - s
            if 0 <= item < count:
                held[item] = stage(item, held.get(item))


def fine_kernel(whose_ref, slot_ref, entry_ref, tiles_ref, cells_ref, left_ref, slope_ref, smooth_ref, out_ref):
    step = pl.program_id(0)
    width = 512
    per_step = out_ref.shape[2] // width
    places, strips = tiles_ref.shape[1:3]
    side = tiles_ref.shape[4]

    def lanes(b):
        return slice(b * width, (b + 1) * width)

    def columns_done(b):
        pair = []
        for i in (b, b + 1):
            entry = entry_ref[slot_ref[step * per_step + i]]
            source, place = entry // strips, entry % strips
            pair += [tiles_ref[source, k, place] for k in range(places)]
        return lax.dot_general(
            left_ref[...],
            jnp.concatenate(pair, axis=0),
            (((1,), (1,)), ((), ())),
            preferred_element_type=F32,
        ).astype(BF)

    def fields(partial):
        partial = [partial[:, :side], partial[:, side:]]
        along_x = jnp.concatenate([p[:side] for p in partial], axis=0)
        along_y = jnp.concatenate([p[side:] for p in partial], axis=0)
        along_x = jnp.dot(along_x, slope_ref[...], preferred_element_type=F32).astype(BF)
        along_y = jnp.dot(along_y, smooth_ref[...], preferred_element_type=F32).astype(BF)
        past = jnp.zeros((SUB, side), BF)
        tables = []
        for i in range(2):
            x, y = (a[i * side : (i + 1) * side] for a in (along_x, along_y))
            four = (x[:, :side], y[:, :side], x[:, side:], y[:, side:])
            tables.append(two_halves([jnp.concatenate([f, past], axis=0) for f in four]))
        return tables

    def gather_rows(b, table):
        row, _ = split_columns(cells_ref[0, 0:1, lanes(b)], cells_ref[0, 1:2, lanes(b)])
        hot = jnp.concatenate(onehot_tiles(row, 2 * side // SUB, width), axis=0)
        return jnp.dot(table, hot, preferred_element_type=F32)

    def gather_columns(b, found):
        _, column = split_columns(cells_ref[0, 0:1, lanes(b)], cells_ref[0, 1:2, lanes(b)])
        out_ref[0, :, lanes(b)] = corner_values(found, column).astype(BF)

    partial, tables, found = {}, {}, {}
    for turn in range(per_step + 4):
        if turn < per_step and turn % 2 == 0:
            partial[turn] = columns_done(turn)
        b = turn - 2
        if 0 <= b < per_step and b % 2 == 0:
            tables[b], tables[b + 1] = fields(partial.pop(b))
        b = turn - 3
        if 0 <= b < per_step:
            found[b] = gather_rows(b, tables.pop(b))
        b = turn - 4
        if 0 <= b < per_step:
            gather_columns(b, found.pop(b))


def long_kernel(whose_ref, start_ref, map_ref, cells_ref, out_ref):
    step = pl.program_id(0)
    width = 512
    per_step = out_ref.shape[2] // width
    extent = map_ref.shape[1]
    side = 128
    rows = side + SUB

    def lanes(b):
        return slice(b * width, (b + 1) * width)

    def bases(b):
        block = step * per_step + b
        row_start = start_ref[0, block]
        col_start = start_ref[1, block]
        row_base = jnp.minimum(row_start // side, extent // side - 2) * side
        col_base = jnp.minimum(col_start // SUB, (extent - rows) // SUB) * SUB
        return row_start, pl.multiple_of(row_base, side), col_start, pl.multiple_of(col_base, SUB)

    def place(b):
        _, _, col_start, col_base = bases(b)
        column = cells_ref[0, 3:4, lanes(b)] + (col_start - col_base).astype(F32)
        return split_columns(cells_ref[0, 2:3, lanes(b)], column)

    def gather_rows(b, _):
        row_start, row_base, _, col_base = bases(b)
        offset = row_start - row_base
        parts = []
        for turn in ((2 * side - offset) & (2 * side - 1), 2 * side - 1 - offset):
            for i in range(2):
                window = map_ref[i, pl.ds(col_base, rows), pl.ds(row_base, 2 * side)]
                parts.append(pltpu.roll(window, turn, axis=1)[:, :side])
        row, _ = place(b)
        hot = jnp.concatenate(onehot_tiles(row, 2 * side // SUB, width), axis=0)
        return jnp.dot(two_halves(parts), hot, preferred_element_type=F32)

    def gather_columns(b, found):
        _, column = place(b)
        out_ref[0, :, lanes(b)] = corner_values(found, column).astype(BF)

    pipelined(per_step, (gather_rows, gather_columns))


def pick_kernel(wanted_ref, *refs):
    sources, out_ref = refs[:-1], refs[-1]
    step = pl.program_id(0)
    count, planes, places = out_ref.shape[:3]
    each = places // len(sources)
    for i in range(count):
        for k in range(planes):
            for j in range(places):
                tile = wanted_ref[step * count + i, k * places + j]
                out_ref[i, k, j] = sources[j // each][k, tile]


def weighted(corners, p, q):
    sub = lax.broadcasted_iota(jnp.int32, corners.shape, 0)
    p, q = jnp.broadcast_to(p, corners.shape), jnp.broadcast_to(q, corners.shape)
    row = jnp.where(sub < 4, 1.0 - p, p).astype(BF).astype(F32)
    column = jnp.where(sub % 2 == 0, 1.0 - q, q)
    return corners * row * column


def lens_shift(previous, target):
    shift = 0.0
    for earlier, deflection in enumerate(previous):
        shift = shift - (target - earlier) / target * deflection
    return shift


def final_kernel(fine_ref, long_ref, frac_ref, deflection_ref, source_ref):
    planes = fine_ref.shape[0]
    found = []
    for k in range(planes):
        at = frac_ref[k]
        p, q, p2, q2 = (at[i : i + 1] for i in range(4))
        if k > 0:
            shift = lens_shift(found, k)
            sx, sy = shift[0:1], shift[2:3]
            p, q, p2, q2 = p + sx, q + sy, p2 + sx / RATIO, q2 + sy / RATIO
        terms = weighted(fine_ref[k].astype(F32), p, q) + weighted(long_ref[k].astype(F32), p2, q2)
        terms = terms + pltpu.roll(terms, 4, axis=0)
        terms = terms + pltpu.roll(terms, 7, axis=0)
        found.append(terms)
        deflection_ref[k, 0:1] = terms[0:1]
        deflection_ref[k, 1:2] = terms[2:3]
    shift = lens_shift(found, planes)
    source_ref[0:1] = shift[0:1]
    source_ref[1:2] = shift[2:3]


def per_device(
    tile_density,
    long_maps,
    map_owner,
    tile_lists,
    block_slots,
    block_windows,
    fine_cells,
    long_cells,
    fractions,
):
    my_row = lax.axis_index("rays")
    plane = lax.axis_index("planes")
    planes, tile_dev, strip, side = tile_density.shape
    extent = long_maps.shape[2]
    list_len = tile_lists.shape[2]
    rays_here = fine_cells.shape[2]
    blocks = block_slots.shape[1]
    ray_count = lax.axis_size("rays")
    level = ray_count // ZG
    my_z, my_xy = my_row // level, my_row % level
    flat_groups = [[z * level + i for i in range(level)] for z in range(ZG)]

    def moved(x, stride, d):
        pairs = [(r, r + ((r // stride + d) % ZG - r // stride % ZG) * stride) for r in range(ray_count)]
        return lax.ppermute(x, "rays", pairs)

    def along_z(x, d):
        return moved(x, level, d)

    def exchange_flat(x):
        return lax.all_to_all(x, "rays", 0, 0, tiled=True, axis_index_groups=flat_groups)

    own_map = lax.dynamic_index_in_dim(long_maps[0], plane, 0, keepdims=False)
    own_map = own_map.transpose(1, 2, 0).reshape(level, 2 * extent // level, extent)
    owner = lax.dynamic_index_in_dim(map_owner, plane, 0, keepdims=False)
    tile_density, own_map = lax.optimization_barrier((tile_density, own_map))
    pieces = exchange_flat(own_map)
    piece = lax.dynamic_index_in_dim(pieces, owner % level, 0, keepdims=False)

    column = [tile_density] + [along_z(tile_density, d) for d in range(1, ZG)]

    level_lists = lax.dynamic_slice(tile_lists, (my_z * level, 0, 0), (level, planes, list_len))
    owners = level_lists // tile_dev
    key = jnp.arange(list_len, dtype=jnp.int32) * tile_dev + level_lists % tile_dev
    column_owner = (my_z - jnp.arange(ZG, dtype=jnp.int32)) % ZG * level + my_xy
    mine = owners[:, :, None, :] == column_owner[None, None, :, None]
    first = jnp.min(jnp.where(mine, key[:, :, None, :], tile_dev * list_len), axis=3) % tile_dev
    last = jnp.max(jnp.where(mine, key[:, :, None, :], 0), axis=3) % tile_dev
    wanted = jnp.stack([first, last], axis=3).reshape(level, planes * ZG * 2)
    outgoing = pl.pallas_call(
        pick_kernel,
        out_shape=jax.ShapeDtypeStruct((level, planes, ZG * 2, strip, side), BF),
        grid_spec=pltpu.PrefetchScalarGridSpec(
            num_scalar_prefetch=1,
            grid=(level // 2,),
            in_specs=[pl.BlockSpec(memory_space=pltpu.VMEM) for _ in column],
            out_specs=pl.BlockSpec((2, planes, ZG * 2, strip, side), lambda g, *_: (g, 0, 0, 0, 0)),
        ),
        name="pick_strips",
    )(wanted, *column)

    block_slots, block_windows, fine_cells, long_cells, _ = lax.optimization_barrier(
        (block_slots, block_windows, fine_cells, long_cells, own_map)
    )
    small = jnp.concatenate(
        [block_slots[:, None, :], block_windows // SUB, block_windows % SUB], axis=1
    ).reshape(planes, 1, 5 * blocks)
    small = jnp.pad(small, ((0, 0), (0, 3), (0, 128 - 5 * blocks)))
    cells = jnp.concatenate([fine_cells, long_cells], axis=1)
    ray_info = jnp.concatenate([cells, small], axis=2).astype(BF)
    arrived = [lax.dynamic_index_in_dim(ray_info, plane, 0, keepdims=False)]
    for d in range(1, planes):
        pairs = [(i, (i + d) % planes) for i in range(planes)]
        sent = lax.dynamic_index_in_dim(ray_info, (plane + d) % planes, 0, keepdims=False)
        arrived.append(lax.ppermute(sent, "planes", pairs))
    arrived = jnp.stack(arrived)
    outgoing, piece, arrived = lax.optimization_barrier((outgoing, piece, arrived))
    cells = arrived[:, :, :rays_here].astype(F32)
    small = arrived[:, 0, rays_here : rays_here + 5 * blocks].astype(jnp.int32)
    small = small.reshape(planes, 5, blocks)
    turn = (plane - jnp.arange(planes)) % planes
    small = jnp.sum(
        jnp.where(turn[:, None] == jnp.arange(planes), 1, 0)[:, :, None, None] * small[None], axis=1
    )
    slots = small[:, 0].reshape(planes * blocks)
    starts = (small[:, 1:3] * SUB + small[:, 3:5]).transpose(1, 0, 2).reshape(2, planes * blocks)
    whose = plane.reshape(1)

    incoming = lax.all_to_all(
        outgoing.reshape(level * planes, ZG * 2, strip, side),
        ("rays", "planes"),
        0,
        0,
        tiled=True,
        axis_index_groups=[
            list(range(z * level * planes, (z + 1) * level * planes)) for z in range(ZG)
        ],
    ).reshape(level, planes, ZG * 2, strip, side)

    distance = (my_z - owner // level) % ZG
    chosen = piece
    for d in range(1, ZG):
        chosen = jnp.where(distance == d, along_z(piece, d), chosen)

    my_list = lax.dynamic_slice(tile_lists, (my_row, plane, 0), (1, 1, list_len))[0, 0]
    my_owner = my_list // tile_dev
    place = jnp.arange(list_len, dtype=jnp.int32)
    repeat = (my_owner[:, None] == my_owner[None, :]) & (place[:, None] > place[None, :])
    rank = jnp.max(repeat.astype(jnp.int32), axis=1)
    entry = my_owner % level * (2 * ZG) + (my_z - my_owner // level) % ZG * 2 + rank

    copies = jnp.broadcast_to(chosen[None], (level, *chosen.shape))
    copies, incoming = lax.optimization_barrier((copies, incoming))
    whole = exchange_flat(copies)
    whole = whole.reshape(2, extent, extent)

    smooth_table, slope_table = kernel_tables(side)
    left = jnp.concatenate([smooth_table, slope_table], axis=0)
    halves = 2
    wide = rays_here // halves
    vmem = pl.BlockSpec(memory_space=pltpu.VMEM)
    params = pltpu.CompilerParams(vmem_limit_bytes=48 << 20)

    def cell_spec():
        return pl.BlockSpec(
            (1, 4, wide),
            lambda g, whose, *_: ((whose[0] + planes - g // halves) % planes, 0, g % halves),
        )

    fine_corners = pl.pallas_call(
        fine_kernel,
        out_shape=jax.ShapeDtypeStruct((planes, 8, rays_here), BF),
        grid_spec=pltpu.PrefetchScalarGridSpec(
            num_scalar_prefetch=3,
            grid=(planes * halves,),
            in_specs=[vmem, cell_spec(), vmem, vmem, vmem],
            out_specs=pl.BlockSpec((1, 8, wide), lambda g, *_: (g // halves, 0, g % halves)),
        ),
        compiler_params=params,
        name="fine_gather",
    )(whose, slots, entry, incoming, cells, left, with_next(slope_table), with_next(smooth_table))
    fine_corners, whole = lax.optimization_barrier((fine_corners, whole))
    fine_corners = lax.all_to_all(fine_corners, "planes", 0, 0, tiled=True)
    long_corners = pl.pallas_call(
        long_kernel,
        out_shape=jax.ShapeDtypeStruct((planes, 8, rays_here), BF),
        grid_spec=pltpu.PrefetchScalarGridSpec(
            num_scalar_prefetch=2,
            grid=(planes * halves,),
            in_specs=[vmem, cell_spec()],
            out_specs=pl.BlockSpec((1, 8, wide), lambda g, *_: (g // halves, 0, g % halves)),
        ),
        compiler_params=params,
        name="long_gather",
    )(whose, starts, whole, cells)
    long_corners, fine_corners = lax.optimization_barrier((long_corners, fine_corners))
    long_corners = lax.all_to_all(long_corners, "planes", 0, 0, tiled=True)
    part = 2048
    return tuple(
        pl.pallas_call(
            final_kernel,
            out_shape=(
                jax.ShapeDtypeStruct((planes, 2, rays_here), F32),
                jax.ShapeDtypeStruct((2, rays_here), F32),
            ),
            grid=(rays_here // part,),
            in_specs=[
                pl.BlockSpec((planes, 8, part), lambda g: (0, 0, g)),
                pl.BlockSpec((planes, 8, part), lambda g: (0, 0, g)),
                pl.BlockSpec((planes, 4, part), lambda g: (0, 0, g)),
            ],
            out_specs=(
                pl.BlockSpec((planes, 2, part), lambda g: (0, 0, g)),
                pl.BlockSpec((2, part), lambda g: (0, g)),
            ),
            name="lens_sum",
        )(fine_corners, long_corners, fractions)
    )


def solution(mesh):
    return jax.shard_map(
        per_device,
        mesh=mesh,
        in_specs=(
            P(None, "rays", "planes", None),
            P("rays", None, None, None, None),
            P(),
            P(),
            P(None, ("rays", "planes")),
            P(None, None, ("rays", "planes")),
            P(None, None, ("rays", "planes")),
            P(None, None, ("rays", "planes")),
            P(None, None, ("rays", "planes")),
        ),
        out_specs=(P(None, None, ("rays", "planes")), P(None, ("rays", "planes"))),
        check_vma=False,
    )
```

```python
import jax
import jax.numpy as jnp
from jax import lax
from jax.experimental import pallas as pl
from jax.experimental.pallas import tpu as pltpu
from jax.sharding import PartitionSpec as P

RATIO = 16
BF = jnp.bfloat16
F32 = jnp.float32
SUB = 16
ZG = 4
TAPS = 6
HALF = 64


def kernel_tables(side):
    indices = jnp.arange(side, dtype=jnp.int32)
    offset = (indices[:, None] - indices[None, :]).astype(F32)
    tap_offsets = jnp.arange(-TAPS, TAPS + 1, dtype=jnp.int32).astype(F32)
    tap_total = jnp.sum(jnp.exp(-tap_offsets * tap_offsets / 8.0))
    inside = jnp.abs(offset) <= TAPS
    weight = jnp.where(inside, jnp.exp(-offset * offset / 8.0), 0.0) / tap_total
    smooth_table = weight.astype(BF)
    slope_table = (6.0 * offset * weight / 4.0).astype(BF)
    return (smooth_table, slope_table)


def with_next(table):
    following = jnp.concatenate([table[1:], jnp.zeros_like(table[:1])], axis=0)
    return jnp.concatenate([table.T, following.T], axis=1)


def onehot_tiles(row, tiles, width):
    wide = jnp.broadcast_to(row, (SUB, width)).astype(BF)
    place = lax.broadcasted_iota(jnp.int32, (SUB, width), 0).astype(F32)
    one = jnp.ones((SUB, width), BF)
    zero = jnp.zeros((SUB, width), BF)
    return [
        jnp.where(wide == (place + float(SUB * t)).astype(BF), one, zero) for t in range(tiles)
    ]


def two_halves(parts):
    return jnp.concatenate(
        [jnp.concatenate([p[: HALF + SUB], p[HALF:]], axis=1) for p in parts], axis=0
    )


def split_columns(row, column):
    upper = jnp.where(column >= float(HALF), 1.0, 0.0)
    return row + 2 * HALF * upper, column - HALF * upper


def corner_values(found, columns):
    rows, width = found.shape[0] // 4, found.shape[1]
    lane = 128
    half = 2 * lane
    results = []
    for h in range(width // half):
        lanes = slice(h * half, (h + 1) * half)
        column = columns[:, lanes]
        tile_of = [jnp.floor((column + step) * (1.0 / SUB)) for step in (0.0, 1.0)]
        wide = [jnp.broadcast_to(t, (SUB, half)).astype(BF) for t in tile_of]
        kept = [[None, None] for _ in range(4)]
        for t in range(rows // SUB):
            hit = [w == float(t) for w in wide]
            for i in range(4):
                low = found[i * rows + t * SUB : i * rows + (t + 1) * SUB, lanes].astype(BF)
                for s in range(2):
                    kept[i][s] = low if t == 0 else jnp.where(hit[s], low, kept[i][s])
        inner = [
            jnp.broadcast_to(column + s - SUB * tile_of[s], (8, half)).astype(jnp.int32)
            for s in range(2)
        ]
        for w in range(half // lane):
            cut = slice(w * lane, (w + 1) * lane)
            sub = lax.broadcasted_iota(jnp.int32, (8, lane), 0)
            value = None
            for s in range(2):
                row = inner[s][:, cut]
                upper, row = row >= 8, row & 7
                for i in range(4):
                    both = kept[i][s][:, cut].astype(F32)
                    one = jnp.where(upper, both[8:], both[:8])
                    one = jnp.take_along_axis(one, row, axis=0, mode="promise_in_bounds")
                    value = one if value is None else jnp.where(sub == 2 * i + s, one, value)
            results.append(value)
    return jnp.concatenate(results, axis=1)


def pipelined(count, stages):
    held = {}
    for turn in range(count + len(stages) - 1):
        for s, stage in enumerate(stages):
            item = turn - s
            if 0 <= item < count:
                held[item] = stage(item, held.get(item))


def fine_kernel(whose_ref, slot_ref, entry_ref, tiles_ref, cells_ref, left_ref, slope_ref, smooth_ref, out_ref):
    step = pl.program_id(0)
    width = 512
    per_step = out_ref.shape[2] // width
    places, strips = tiles_ref.shape[1:3]
    side = tiles_ref.shape[4]

    def lanes(b):
        return slice(b * width, (b + 1) * width)

    def columns_done(b):
        pair = []
        for i in (b, b + 1):
            entry = entry_ref[slot_ref[step * per_step + i]]
            source, place = entry // strips, entry % strips
            pair += [tiles_ref[source, k, place] for k in range(places)]
        return lax.dot_general(
            left_ref[...],
            jnp.concatenate(pair, axis=0),
            (((1,), (1,)), ((), ())),
            preferred_element_type=F32,
        ).astype(BF)

    def fields(partial):
        partial = [partial[:, :side], partial[:, side:]]
        along_x = jnp.concatenate([p[:side] for p in partial], axis=0)
        along_y = jnp.concatenate([p[side:] for p in partial], axis=0)
        along_x = jnp.dot(along_x, slope_ref[...], preferred_element_type=F32).astype(BF)
        along_y = jnp.dot(along_y, smooth_ref[...], preferred_element_type=F32).astype(BF)
        past = jnp.zeros((SUB, side), BF)
        tables = []
        for i in range(2):
            x, y = (a[i * side : (i + 1) * side] for a in (along_x, along_y))
            four = (x[:, :side], y[:, :side], x[:, side:], y[:, side:])
            tables.append(two_halves([jnp.concatenate([f, past], axis=0) for f in four]))
        return tables

    def gather_rows(b, table):
        row, _ = split_columns(cells_ref[0, 0:1, lanes(b)], cells_ref[0, 1:2, lanes(b)])
        hot = jnp.concatenate(onehot_tiles(row, 2 * side // SUB, width), axis=0)
        return jnp.dot(table, hot, preferred_element_type=F32)

    def gather_columns(b, found):
        _, column = split_columns(cells_ref[0, 0:1, lanes(b)], cells_ref[0, 1:2, lanes(b)])
        out_ref[0, :, lanes(b)] = corner_values(found, column).astype(BF)

    partial, tables, found = {}, {}, {}
    for turn in range(per_step + 4):
        if turn < per_step and turn % 2 == 0:
            partial[turn] = columns_done(turn)
        b = turn - 2
        if 0 <= b < per_step and b % 2 == 0:
            tables[b], tables[b + 1] = fields(partial.pop(b))
        b = turn - 3
        if 0 <= b < per_step:
            found[b] = gather_rows(b, tables.pop(b))
        b = turn - 4
        if 0 <= b < per_step:
            gather_columns(b, found.pop(b))


def long_kernel(whose_ref, start_ref, map_ref, cells_ref, out_ref):
    step = pl.program_id(0)
    width = 512
    per_step = out_ref.shape[2] // width
    extent = map_ref.shape[1]
    side = 128
    rows = side + SUB

    def lanes(b):
        return slice(b * width, (b + 1) * width)

    def bases(b):
        block = step * per_step + b
        row_start = start_ref[0, block]
        col_start = start_ref[1, block]
        row_base = jnp.minimum(row_start // side, extent // side - 2) * side
        col_base = jnp.minimum(col_start // SUB, (extent - rows) // SUB) * SUB
        return row_start, pl.multiple_of(row_base, side), col_start, pl.multiple_of(col_base, SUB)

    def place(b):
        _, _, col_start, col_base = bases(b)
        column = cells_ref[0, 3:4, lanes(b)] + (col_start - col_base).astype(F32)
        return split_columns(cells_ref[0, 2:3, lanes(b)], column)

    def gather_rows(b, _):
        row_start, row_base, _, col_base = bases(b)
        offset = row_start - row_base
        parts = []
        for turn in ((2 * side - offset) & (2 * side - 1), 2 * side - 1 - offset):
            for i in range(2):
                window = map_ref[i, pl.ds(col_base, rows), pl.ds(row_base, 2 * side)]
                parts.append(pltpu.roll(window, turn, axis=1)[:, :side])
        row, _ = place(b)
        hot = jnp.concatenate(onehot_tiles(row, 2 * side // SUB, width), axis=0)
        return jnp.dot(two_halves(parts), hot, preferred_element_type=F32)

    def gather_columns(b, found):
        _, column = place(b)
        out_ref[0, :, lanes(b)] = corner_values(found, column).astype(BF)

    pipelined(per_step, (gather_rows, gather_columns))


def pick_kernel(wanted_ref, *refs):
    sources, out_ref = refs[:-1], refs[-1]
    step = pl.program_id(0)
    count, planes, places = out_ref.shape[:3]
    each = places // len(sources)
    for i in range(count):
        for k in range(planes):
            for j in range(places):
                tile = wanted_ref[step * count + i, k * places + j]
                out_ref[i, k, j] = sources[j // each][k, tile]


def weighted(corners, p, q):
    sub = lax.broadcasted_iota(jnp.int32, corners.shape, 0)
    p, q = jnp.broadcast_to(p, corners.shape), jnp.broadcast_to(q, corners.shape)
    row = jnp.where(sub < 4, 1.0 - p, p).astype(BF).astype(F32)
    column = jnp.where(sub % 2 == 0, 1.0 - q, q)
    return corners * row * column


def lens_shift(previous, target):
    shift = 0.0
    for earlier, deflection in enumerate(previous):
        shift = shift - (target - earlier) / target * deflection
    return shift


def final_kernel(fine_ref, long_ref, frac_ref, deflection_ref, source_ref):
    planes = fine_ref.shape[0]
    found = []
    for k in range(planes):
        at = frac_ref[k]
        p, q, p2, q2 = (at[i : i + 1] for i in range(4))
        if k > 0:
            shift = lens_shift(found, k)
            sx, sy = shift[0:1], shift[2:3]
            p, q, p2, q2 = p + sx, q + sy, p2 + sx / RATIO, q2 + sy / RATIO
        terms = weighted(fine_ref[k].astype(F32), p, q) + weighted(long_ref[k].astype(F32), p2, q2)
        terms = terms + pltpu.roll(terms, 4, axis=0)
        terms = terms + pltpu.roll(terms, 7, axis=0)
        found.append(terms)
        deflection_ref[k, 0:1] = terms[0:1]
        deflection_ref[k, 1:2] = terms[2:3]
    shift = lens_shift(found, planes)
    source_ref[0:1] = shift[0:1]
    source_ref[1:2] = shift[2:3]


def per_device(
    tile_density,
    long_maps,
    map_owner,
    tile_lists,
    block_slots,
    block_windows,
    fine_cells,
    long_cells,
    fractions,
):
    my_row = lax.axis_index("rays")
    plane = lax.axis_index("planes")
    planes, tile_dev, strip, side = tile_density.shape
    extent = long_maps.shape[2]
    list_len = tile_lists.shape[2]
    rays_here = fine_cells.shape[2]
    blocks = block_slots.shape[1]
    ray_count = lax.axis_size("rays")
    level = ray_count // ZG
    my_z, my_xy = my_row // level, my_row % level
    flat_groups = [[z * level + i for i in range(level)] for z in range(ZG)]

    def moved(x, stride, d):
        pairs = [(r, r + ((r // stride + d) % ZG - r // stride % ZG) * stride) for r in range(ray_count)]
        return lax.ppermute(x, "rays", pairs)

    def along_z(x, d):
        return moved(x, level, d)

    def exchange_flat(x):
        return lax.all_to_all(x, "rays", 0, 0, tiled=True, axis_index_groups=flat_groups)

    own_map = lax.dynamic_index_in_dim(long_maps[0], plane, 0, keepdims=False)
    own_map = own_map.transpose(1, 2, 0).reshape(level, 2 * extent // level, extent)
    owner = lax.dynamic_index_in_dim(map_owner, plane, 0, keepdims=False)
    tile_density, own_map = lax.optimization_barrier((tile_density, own_map))
    pieces = exchange_flat(own_map)
    piece = lax.dynamic_index_in_dim(pieces, owner % level, 0, keepdims=False)

    column = [tile_density] + [along_z(tile_density, d) for d in range(1, ZG)]

    level_lists = lax.dynamic_slice(tile_lists, (my_z * level, 0, 0), (level, planes, list_len))
    owners = level_lists // tile_dev
    key = jnp.arange(list_len, dtype=jnp.int32) * tile_dev + level_lists % tile_dev
    column_owner = (my_z - jnp.arange(ZG, dtype=jnp.int32)) % ZG * level + my_xy
    mine = owners[:, :, None, :] == column_owner[None, None, :, None]
    first = jnp.min(jnp.where(mine, key[:, :, None, :], tile_dev * list_len), axis=3) % tile_dev
    last = jnp.max(jnp.where(mine, key[:, :, None, :], 0), axis=3) % tile_dev
    wanted = jnp.stack([first, last], axis=3).reshape(level, planes * ZG * 2)
    outgoing = pl.pallas_call(
        pick_kernel,
        out_shape=jax.ShapeDtypeStruct((level, planes, ZG * 2, strip, side), BF),
        grid_spec=pltpu.PrefetchScalarGridSpec(
            num_scalar_prefetch=1,
            grid=(level // 4,),
            in_specs=[pl.BlockSpec(memory_space=pltpu.VMEM) for _ in column],
            out_specs=pl.BlockSpec((4, planes, ZG * 2, strip, side), lambda g, *_: (g, 0, 0, 0, 0)),
        ),
        name="pick_strips",
    )(wanted, *column)

    block_slots, block_windows, fine_cells, long_cells, _ = lax.optimization_barrier(
        (block_slots, block_windows, fine_cells, long_cells, own_map)
    )
    small = jnp.concatenate(
        [block_slots[:, None, :], block_windows // SUB, block_windows % SUB], axis=1
    ).reshape(planes, 1, 5 * blocks)
    small = jnp.pad(small, ((0, 0), (0, 3), (0, 128 - 5 * blocks)))
    cells = jnp.concatenate([fine_cells, long_cells], axis=1)
    ray_info = jnp.concatenate([cells, small], axis=2).astype(BF)
    arrived = [lax.dynamic_index_in_dim(ray_info, plane, 0, keepdims=False)]
    for d in range(1, planes):
        pairs = [(i, (i + d) % planes) for i in range(planes)]
        sent = lax.dynamic_index_in_dim(ray_info, (plane + d) % planes, 0, keepdims=False)
        arrived.append(lax.ppermute(sent, "planes", pairs))
    arrived = jnp.stack(arrived)
    outgoing, piece, arrived = lax.optimization_barrier((outgoing, piece, arrived))
    cells = arrived[:, :, :rays_here].astype(F32)
    small = arrived[:, 0, rays_here : rays_here + 5 * blocks].astype(jnp.int32)
    small = small.reshape(planes, 5, blocks)
    turn = (plane - jnp.arange(planes)) % planes
    small = jnp.sum(
        jnp.where(turn[:, None] == jnp.arange(planes), 1, 0)[:, :, None, None] * small[None], axis=1
    )
    slots = small[:, 0].reshape(planes * blocks)
    starts = (small[:, 1:3] * SUB + small[:, 3:5]).transpose(1, 0, 2).reshape(2, planes * blocks)
    whose = plane.reshape(1)

    incoming = lax.all_to_all(
        outgoing.reshape(level * planes, ZG * 2, strip, side),
        ("rays", "planes"),
        0,
        0,
        tiled=True,
        axis_index_groups=[
            list(range(z * level * planes, (z + 1) * level * planes)) for z in range(ZG)
        ],
    ).reshape(level, planes, ZG * 2, strip, side)

    distance = (my_z - owner // level) % ZG
    chosen = piece
    for d in range(1, ZG):
        chosen = jnp.where(distance == d, along_z(piece, d), chosen)

    my_list = lax.dynamic_slice(tile_lists, (my_row, plane, 0), (1, 1, list_len))[0, 0]
    my_owner = my_list // tile_dev
    place = jnp.arange(list_len, dtype=jnp.int32)
    repeat = (my_owner[:, None] == my_owner[None, :]) & (place[:, None] > place[None, :])
    rank = jnp.max(repeat.astype(jnp.int32), axis=1)
    entry = my_owner % level * (2 * ZG) + (my_z - my_owner // level) % ZG * 2 + rank

    copies = jnp.broadcast_to(chosen[None], (level, *chosen.shape))
    copies, incoming = lax.optimization_barrier((copies, incoming))
    whole = exchange_flat(copies)
    whole = whole.reshape(2, extent, extent)

    smooth_table, slope_table = kernel_tables(side)
    left = jnp.concatenate([smooth_table, slope_table], axis=0)
    halves = 1
    wide = rays_here // halves
    vmem = pl.BlockSpec(memory_space=pltpu.VMEM)
    params = pltpu.CompilerParams(vmem_limit_bytes=48 << 20)

    def cell_spec():
        return pl.BlockSpec(
            (1, 4, wide),
            lambda g, whose, *_: ((whose[0] + planes - g // halves) % planes, 0, g % halves),
        )

    fine_corners = pl.pallas_call(
        fine_kernel,
        out_shape=jax.ShapeDtypeStruct((planes, 8, rays_here), BF),
        grid_spec=pltpu.PrefetchScalarGridSpec(
            num_scalar_prefetch=3,
            grid=(planes * halves,),
            in_specs=[vmem, cell_spec(), vmem, vmem, vmem],
            out_specs=pl.BlockSpec((1, 8, wide), lambda g, *_: (g // halves, 0, g % halves)),
        ),
        compiler_params=params,
        name="fine_gather",
    )(whose, slots, entry, incoming, cells, left, with_next(slope_table), with_next(smooth_table))
    fine_corners, whole = lax.optimization_barrier((fine_corners, whole))
    fine_corners = lax.all_to_all(fine_corners, "planes", 0, 0, tiled=True)
    long_corners = pl.pallas_call(
        long_kernel,
        out_shape=jax.ShapeDtypeStruct((planes, 8, rays_here), BF),
        grid_spec=pltpu.PrefetchScalarGridSpec(
            num_scalar_prefetch=2,
            grid=(planes * halves,),
            in_specs=[vmem, cell_spec()],
            out_specs=pl.BlockSpec((1, 8, wide), lambda g, *_: (g // halves, 0, g % halves)),
        ),
        compiler_params=params,
        name="long_gather",
    )(whose, starts, whole, cells)
    long_corners, fine_corners = lax.optimization_barrier((long_corners, fine_corners))
    long_corners = lax.all_to_all(long_corners, "planes", 0, 0, tiled=True)
    part = 4096
    return tuple(
        pl.pallas_call(
            final_kernel,
            out_shape=(
                jax.ShapeDtypeStruct((planes, 2, rays_here), F32),
                jax.ShapeDtypeStruct((2, rays_here), F32),
            ),
            grid=(rays_here // part,),
            in_specs=[
                pl.BlockSpec((planes, 8, part), lambda g: (0, 0, g)),
                pl.BlockSpec((planes, 8, part), lambda g: (0, 0, g)),
                pl.BlockSpec((planes, 4, part), lambda g: (0, 0, g)),
            ],
            out_specs=(
                pl.BlockSpec((planes, 2, part), lambda g: (0, 0, g)),
                pl.BlockSpec((2, part), lambda g: (0, g)),
            ),
            name="lens_sum",
        )(fine_corners, long_corners, fractions)
    )


def solution(mesh):
    return jax.shard_map(
        per_device,
        mesh=mesh,
        in_specs=(
            P(None, "rays", "planes", None),
            P("rays", None, None, None, None),
            P(),
            P(),
            P(None, ("rays", "planes")),
            P(None, None, ("rays", "planes")),
            P(None, None, ("rays", "planes")),
            P(None, None, ("rays", "planes")),
            P(None, None, ("rays", "planes")),
        ),
        out_specs=(P(None, None, ("rays", "planes")), P(None, ("rays", "planes"))),
        check_vma=False,
    )
```

```python
import jax
import jax.numpy as jnp
from jax import lax
from jax.experimental import pallas as pl
from jax.experimental.pallas import tpu as pltpu
from jax.sharding import PartitionSpec as P

RATIO = 16
BF = jnp.bfloat16
F32 = jnp.float32
SUB = 16
ZG = 4
TAPS = 6
HALF = 64


def kernel_tables(side):
    indices = jnp.arange(side, dtype=jnp.int32)
    offset = (indices[:, None] - indices[None, :]).astype(F32)
    tap_offsets = jnp.arange(-TAPS, TAPS + 1, dtype=jnp.int32).astype(F32)
    tap_total = jnp.sum(jnp.exp(-tap_offsets * tap_offsets / 8.0))
    inside = jnp.abs(offset) <= TAPS
    weight = jnp.where(inside, jnp.exp(-offset * offset / 8.0), 0.0) / tap_total
    smooth_table = weight.astype(BF)
    slope_table = (6.0 * offset * weight / 4.0).astype(BF)
    return (smooth_table, slope_table)


def with_next(table):
    following = jnp.concatenate([table[1:], jnp.zeros_like(table[:1])], axis=0)
    return jnp.concatenate([table.T, following.T], axis=1)


def onehot_tiles(row, tiles, width):
    wide = jnp.broadcast_to(row, (SUB, width)).astype(BF)
    place = lax.broadcasted_iota(jnp.int32, (SUB, width), 0).astype(F32)
    one = jnp.ones((SUB, width), BF)
    zero = jnp.zeros((SUB, width), BF)
    return [
        jnp.where(wide == (place + float(SUB * t)).astype(BF), one, zero) for t in range(tiles)
    ]


def two_halves(parts):
    return jnp.concatenate(
        [jnp.concatenate([p[: HALF + SUB], p[HALF:]], axis=1) for p in parts], axis=0
    )


def split_columns(row, column):
    upper = jnp.where(column >= float(HALF), 1.0, 0.0)
    return row + 2 * HALF * upper, column - HALF * upper


def corner_values(found, columns):
    rows, width = found.shape[0] // 4, found.shape[1]
    lane = 128
    half = 2 * lane
    results = []
    for h in range(width // half):
        lanes = slice(h * half, (h + 1) * half)
        column = columns[:, lanes]
        tile_of = [jnp.floor((column + step) * (1.0 / SUB)) for step in (0.0, 1.0)]
        wide = [jnp.broadcast_to(t, (SUB, half)).astype(BF) for t in tile_of]
        kept = [[None, None] for _ in range(4)]
        for t in range(rows // SUB):
            hit = [w == float(t) for w in wide]
            for i in range(4):
                low = found[i * rows + t * SUB : i * rows + (t + 1) * SUB, lanes].astype(BF)
                for s in range(2):
                    kept[i][s] = low if t == 0 else jnp.where(hit[s], low, kept[i][s])
        inner = [
            jnp.broadcast_to(column + s - SUB * tile_of[s], (8, half)).astype(jnp.int32)
            for s in range(2)
        ]
        for w in range(half // lane):
            cut = slice(w * lane, (w + 1) * lane)
            sub = lax.broadcasted_iota(jnp.int32, (8, lane), 0)
            value = None
            for s in range(2):
                row = inner[s][:, cut]
                upper, row = row >= 8, row & 7
                for i in range(4):
                    both = kept[i][s][:, cut].astype(F32)
                    one = jnp.where(upper, both[8:], both[:8])
                    one = jnp.take_along_axis(one, row, axis=0, mode="promise_in_bounds")
                    value = one if value is None else jnp.where(sub == 2 * i + s, one, value)
            results.append(value)
    return jnp.concatenate(results, axis=1)


def pipelined(count, stages):
    held = {}
    for turn in range(count + len(stages) - 1):
        for s, stage in enumerate(stages):
            item = turn - s
            if 0 <= item < count:
                held[item] = stage(item, held.get(item))


def fine_kernel(whose_ref, slot_ref, entry_ref, tiles_ref, cells_ref, left_ref, slope_ref, smooth_ref, out_ref):
    step = pl.program_id(0)
    width = 512
    per_step = out_ref.shape[2] // width
    places, strips = tiles_ref.shape[1:3]
    side = tiles_ref.shape[4]

    def lanes(b):
        return slice(b * width, (b + 1) * width)

    def columns_done(b):
        pair = []
        for i in (b, b + 1):
            entry = entry_ref[slot_ref[step * per_step + i]]
            source, place = entry // strips, entry % strips
            pair += [tiles_ref[source, k, place] for k in range(places)]
        return lax.dot_general(
            left_ref[...],
            jnp.concatenate(pair, axis=0),
            (((1,), (1,)), ((), ())),
            preferred_element_type=F32,
        ).astype(BF)

    def fields(partial):
        partial = [partial[:, :side], partial[:, side:]]
        along_x = jnp.concatenate([p[:side] for p in partial], axis=0)
        along_y = jnp.concatenate([p[side:] for p in partial], axis=0)
        along_x = jnp.dot(along_x, slope_ref[...], preferred_element_type=F32).astype(BF)
        along_y = jnp.dot(along_y, smooth_ref[...], preferred_element_type=F32).astype(BF)
        past = jnp.zeros((SUB, side), BF)
        tables = []
        for i in range(2):
            x, y = (a[i * side : (i + 1) * side] for a in (along_x, along_y))
            four = (x[:, :side], y[:, :side], x[:, side:], y[:, side:])
            tables.append(two_halves([jnp.concatenate([f, past], axis=0) for f in four]))
        return tables

    def gather_rows(b, table):
        row, _ = split_columns(cells_ref[0, 0:1, lanes(b)], cells_ref[0, 1:2, lanes(b)])
        hot = jnp.concatenate(onehot_tiles(row, 2 * side // SUB, width), axis=0)
        return jnp.dot(table, hot, preferred_element_type=F32)

    def gather_columns(b, found):
        _, column = split_columns(cells_ref[0, 0:1, lanes(b)], cells_ref[0, 1:2, lanes(b)])
        out_ref[0, :, lanes(b)] = corner_values(found, column).astype(BF)

    partial, tables, found = {}, {}, {}
    for turn in range(per_step + 4):
        if turn < per_step and turn % 2 == 0:
            partial[turn] = columns_done(turn)
        b = turn - 2
        if 0 <= b < per_step and b % 2 == 0:
            tables[b], tables[b + 1] = fields(partial.pop(b))
        b = turn - 3
        if 0 <= b < per_step:
            found[b] = gather_rows(b, tables.pop(b))
        b = turn - 4
        if 0 <= b < per_step:
            gather_columns(b, found.pop(b))


def long_kernel(whose_ref, start_ref, map_ref, cells_ref, out_ref):
    step = pl.program_id(0)
    width = 512
    per_step = out_ref.shape[2] // width
    extent = map_ref.shape[1]
    side = 128
    rows = side + SUB

    def lanes(b):
        return slice(b * width, (b + 1) * width)

    def bases(b):
        block = step * per_step + b
        row_start = start_ref[0, block]
        col_start = start_ref[1, block]
        row_base = jnp.minimum(row_start // side, extent // side - 2) * side
        col_base = jnp.minimum(col_start // SUB, (extent - rows) // SUB) * SUB
        return row_start, pl.multiple_of(row_base, side), col_start, pl.multiple_of(col_base, SUB)

    def place(b):
        _, _, col_start, col_base = bases(b)
        column = cells_ref[0, 3:4, lanes(b)] + (col_start - col_base).astype(F32)
        return split_columns(cells_ref[0, 2:3, lanes(b)], column)

    def gather_rows(b, _):
        row_start, row_base, _, col_base = bases(b)
        offset = row_start - row_base
        parts = []
        for turn in ((2 * side - offset) & (2 * side - 1), 2 * side - 1 - offset):
            for i in range(2):
                window = map_ref[i, pl.ds(col_base, rows), pl.ds(row_base, 2 * side)]
                parts.append(pltpu.roll(window, turn, axis=1)[:, :side])
        row, _ = place(b)
        hot = jnp.concatenate(onehot_tiles(row, 2 * side // SUB, width), axis=0)
        return jnp.dot(two_halves(parts), hot, preferred_element_type=F32)

    def gather_columns(b, found):
        _, column = place(b)
        out_ref[0, :, lanes(b)] = corner_values(found, column).astype(BF)

    pipelined(per_step, (gather_rows, gather_columns))


def pick_kernel(wanted_ref, *refs):
    sources, out_ref = refs[:-1], refs[-1]
    step = pl.program_id(0)
    count, planes, places = out_ref.shape[:3]
    each = places // len(sources)
    for i in range(count):
        for k in range(planes):
            for j in range(places):
                tile = wanted_ref[step * count + i, k * places + j]
                out_ref[i, k, j] = sources[j // each][k, tile]


def weighted(corners, p, q):
    sub = lax.broadcasted_iota(jnp.int32, corners.shape, 0)
    p, q = jnp.broadcast_to(p, corners.shape), jnp.broadcast_to(q, corners.shape)
    row = jnp.where(sub < 4, 1.0 - p, p).astype(BF).astype(F32)
    column = jnp.where(sub % 2 == 0, 1.0 - q, q)
    return corners * row * column


def lens_shift(previous, target):
    shift = 0.0
    for earlier, deflection in enumerate(previous):
        shift = shift - (target - earlier) / target * deflection
    return shift


def final_kernel(whose_ref, fine_ref, long_ref, frac_ref, deflection_ref, source_ref):
    planes = fine_ref.shape[0]
    found = []
    for k in range(planes):
        at = frac_ref[k]
        p, q, p2, q2 = (at[i : i + 1] for i in range(4))
        if k > 0:
            shift = lens_shift(found, k)
            sx, sy = shift[0:1], shift[2:3]
            p, q, p2, q2 = p + sx, q + sy, p2 + sx / RATIO, q2 + sy / RATIO
        terms = weighted(fine_ref[lax.rem(whose_ref[0] + (planes - k), planes)].astype(F32), p, q) + weighted(long_ref[k].astype(F32), p2, q2)
        terms = terms + pltpu.roll(terms, 4, axis=0)
        terms = terms + pltpu.roll(terms, 7, axis=0)
        found.append(terms)
        deflection_ref[k, 0:1] = terms[0:1]
        deflection_ref[k, 1:2] = terms[2:3]
    shift = lens_shift(found, planes)
    source_ref[0:1] = shift[0:1]
    source_ref[1:2] = shift[2:3]


def per_device(
    tile_density,
    long_maps,
    map_owner,
    tile_lists,
    block_slots,
    block_windows,
    fine_cells,
    long_cells,
    fractions,
):
    my_row = lax.axis_index("rays")
    plane = lax.axis_index("planes")
    planes, tile_dev, strip, side = tile_density.shape
    extent = long_maps.shape[2]
    list_len = tile_lists.shape[2]
    rays_here = fine_cells.shape[2]
    blocks = block_slots.shape[1]
    ray_count = lax.axis_size("rays")
    level = ray_count // ZG
    my_z, my_xy = my_row // level, my_row % level
    flat_groups = [[z * level + i for i in range(level)] for z in range(ZG)]

    def moved(x, stride, d):
        pairs = [(r, r + ((r // stride + d) % ZG - r // stride % ZG) * stride) for r in range(ray_count)]
        return lax.ppermute(x, "rays", pairs)

    def along_z(x, d):
        return moved(x, level, d)

    def exchange_flat(x):
        return lax.all_to_all(x, "rays", 0, 0, tiled=True, axis_index_groups=flat_groups)

    own_map = lax.dynamic_index_in_dim(long_maps[0], plane, 0, keepdims=False)
    own_map = own_map.transpose(1, 2, 0).reshape(level, 2 * extent // level, extent)
    owner = lax.dynamic_index_in_dim(map_owner, plane, 0, keepdims=False)
    tile_density, own_map = lax.optimization_barrier((tile_density, own_map))
    pieces = exchange_flat(own_map)
    piece = lax.dynamic_index_in_dim(pieces, owner % level, 0, keepdims=False)

    column = [tile_density] + [along_z(tile_density, d) for d in range(1, ZG)]

    level_lists = lax.dynamic_slice(tile_lists, (my_z * level, 0, 0), (level, planes, list_len))
    owners = level_lists // tile_dev
    key = jnp.arange(list_len, dtype=jnp.int32) * tile_dev + level_lists % tile_dev
    column_owner = (my_z - jnp.arange(ZG, dtype=jnp.int32)) % ZG * level + my_xy
    mine = owners[:, :, None, :] == column_owner[None, None, :, None]
    first = jnp.min(jnp.where(mine, key[:, :, None, :], tile_dev * list_len), axis=3) % tile_dev
    last = jnp.max(jnp.where(mine, key[:, :, None, :], 0), axis=3) % tile_dev
    wanted = jnp.stack([first, last], axis=3).reshape(level, planes * ZG * 2)
    outgoing = pl.pallas_call(
        pick_kernel,
        out_shape=jax.ShapeDtypeStruct((level, planes, ZG * 2, strip, side), BF),
        grid_spec=pltpu.PrefetchScalarGridSpec(
            num_scalar_prefetch=1,
            grid=(level // 4,),
            in_specs=[pl.BlockSpec(memory_space=pltpu.VMEM) for _ in column],
            out_specs=pl.BlockSpec((4, planes, ZG * 2, strip, side), lambda g, *_: (g, 0, 0, 0, 0)),
        ),
        name="pick_strips",
    )(wanted, *column)

    block_slots, block_windows, fine_cells, long_cells, _ = lax.optimization_barrier(
        (block_slots, block_windows, fine_cells, long_cells, own_map)
    )
    small = jnp.concatenate(
        [block_slots[:, None, :], block_windows // SUB, block_windows % SUB], axis=1
    ).reshape(planes, 1, 5 * blocks)
    small = jnp.pad(small, ((0, 0), (0, 3), (0, 128 - 5 * blocks)))
    cells = jnp.concatenate([fine_cells, long_cells], axis=1)
    ray_info = jnp.concatenate([cells, small], axis=2).astype(BF)
    arrived = [lax.dynamic_index_in_dim(ray_info, plane, 0, keepdims=False)]
    for d in range(1, planes):
        pairs = [(i, (i + d) % planes) for i in range(planes)]
        sent = lax.dynamic_index_in_dim(ray_info, (plane + d) % planes, 0, keepdims=False)
        arrived.append(lax.ppermute(sent, "planes", pairs))
    arrived = jnp.stack(arrived)
    outgoing, piece, arrived = lax.optimization_barrier((outgoing, piece, arrived))
    cells = arrived[:, :, :rays_here].astype(F32)
    small = arrived[:, 0, rays_here : rays_here + 5 * blocks].astype(jnp.int32)
    small = small.reshape(planes, 5, blocks)
    turn = (plane - jnp.arange(planes)) % planes
    small = jnp.sum(
        jnp.where(turn[:, None] == jnp.arange(planes), 1, 0)[:, :, None, None] * small[None], axis=1
    )
    slots = small[:, 0].reshape(planes * blocks)
    starts = (small[:, 1:3] * SUB + small[:, 3:5]).transpose(1, 0, 2).reshape(2, planes * blocks)
    whose = plane.reshape(1)

    incoming = lax.all_to_all(
        outgoing.reshape(level * planes, ZG * 2, strip, side),
        ("rays", "planes"),
        0,
        0,
        tiled=True,
        axis_index_groups=[
            list(range(z * level * planes, (z + 1) * level * planes)) for z in range(ZG)
        ],
    ).reshape(level, planes, ZG * 2, strip, side)

    distance = (my_z - owner // level) % ZG
    chosen = piece
    for d in range(1, ZG):
        chosen = jnp.where(distance == d, along_z(piece, d), chosen)

    my_list = lax.dynamic_slice(tile_lists, (my_row, plane, 0), (1, 1, list_len))[0, 0]
    my_owner = my_list // tile_dev
    place = jnp.arange(list_len, dtype=jnp.int32)
    repeat = (my_owner[:, None] == my_owner[None, :]) & (place[:, None] > place[None, :])
    rank = jnp.max(repeat.astype(jnp.int32), axis=1)
    entry = my_owner % level * (2 * ZG) + (my_z - my_owner // level) % ZG * 2 + rank

    copies = jnp.broadcast_to(chosen[None], (level, *chosen.shape))
    copies, incoming = lax.optimization_barrier((copies, incoming))
    whole = exchange_flat(copies)
    whole = whole.reshape(2, extent, extent)

    smooth_table, slope_table = kernel_tables(side)
    left = jnp.concatenate([smooth_table, slope_table], axis=0)
    halves = 1
    wide = rays_here // halves
    vmem = pl.BlockSpec(memory_space=pltpu.VMEM)
    params = pltpu.CompilerParams(vmem_limit_bytes=48 << 20)

    def cell_spec():
        return pl.BlockSpec(
            (1, 4, wide),
            lambda g, whose, *_: ((whose[0] + planes - g // halves) % planes, 0, g % halves),
        )

    fine_corners = pl.pallas_call(
        fine_kernel,
        out_shape=jax.ShapeDtypeStruct((planes, 8, rays_here), BF),
        grid_spec=pltpu.PrefetchScalarGridSpec(
            num_scalar_prefetch=3,
            grid=(planes * halves,),
            in_specs=[vmem, cell_spec(), vmem, vmem, vmem],
            out_specs=pl.BlockSpec((1, 8, wide), lambda g, *_: (g // halves, 0, g % halves)),
        ),
        compiler_params=params,
        name="fine_gather",
    )(whose, slots, entry, incoming, cells, left, with_next(slope_table), with_next(smooth_table))
    back = [lax.dynamic_index_in_dim(fine_corners, plane, 0, keepdims=False)]
    for d in range(1, planes):
        pairs = [(i, (i + d) % planes) for i in range(planes)]
        sent = lax.dynamic_index_in_dim(fine_corners, (plane + d) % planes, 0, keepdims=False)
        back.append(lax.ppermute(sent, "planes", pairs))
    long_corners = pl.pallas_call(
        long_kernel,
        out_shape=jax.ShapeDtypeStruct((planes, 8, rays_here), BF),
        grid_spec=pltpu.PrefetchScalarGridSpec(
            num_scalar_prefetch=2,
            grid=(planes * halves,),
            in_specs=[vmem, cell_spec()],
            out_specs=pl.BlockSpec((1, 8, wide), lambda g, *_: (g // halves, 0, g % halves)),
        ),
        compiler_params=params,
        name="long_gather",
    )(whose, starts, whole, cells)
    long_corners = lax.all_to_all(long_corners, "planes", 0, 0, tiled=True)
    part = 4096
    return tuple(
        pl.pallas_call(
            final_kernel,
            out_shape=(
                jax.ShapeDtypeStruct((planes, 2, rays_here), F32),
                jax.ShapeDtypeStruct((2, rays_here), F32),
            ),
            grid_spec=pltpu.PrefetchScalarGridSpec(
                num_scalar_prefetch=1,
                grid=(rays_here // part,),
                in_specs=[
                    pl.BlockSpec((planes, 8, part), lambda g, *_: (0, 0, g)),
                    pl.BlockSpec((planes, 8, part), lambda g, *_: (0, 0, g)),
                    pl.BlockSpec((planes, 4, part), lambda g, *_: (0, 0, g)),
                ],
                out_specs=(
                    pl.BlockSpec((planes, 2, part), lambda g, *_: (0, 0, g)),
                    pl.BlockSpec((2, part), lambda g, *_: (0, g)),
                ),
            ),
            name="lens_sum",
        )(whose, jnp.stack(back), long_corners, fractions)
    )


def solution(mesh):
    return jax.shard_map(
        per_device,
        mesh=mesh,
        in_specs=(
            P(None, "rays", "planes", None),
            P("rays", None, None, None, None),
            P(),
            P(),
            P(None, ("rays", "planes")),
            P(None, None, ("rays", "planes")),
            P(None, None, ("rays", "planes")),
            P(None, None, ("rays", "planes")),
            P(None, None, ("rays", "planes")),
        ),
        out_specs=(P(None, None, ("rays", "planes")), P(None, ("rays", "planes"))),
        check_vma=False,
    )
```
